32 devices in a mesh: seq: 8 (over y, x, core), chan: 4 (over z).
Axes of the slice: x: 2, y: 2, z: 4, core: 2. Of those that a mesh axis runs over, the one named last changes fastest.
Arguments:
- hidden: bfloat16 [4096, 4096], P('seq', 'chan'), may hold values from -6 to 6
- norm_gain: float32 [2048], replicated, may hold values from 0.25 to 1.75
- w_values: bfloat16 [2048, 4096], P(None, 'chan'), may hold values from -0.125 to 0.125
- w_gates: bfloat16 [2048, 4096], P(None, 'chan'), may hold values from -0.125 to 0.125
- w_control: bfloat16 [2048, 320], replicated, may hold values from -0.046875 to 0.046875
- dt_bias: float32 [64], replicated, may hold values from -1 to 1
- decay_total: float32 [64], replicated, may hold values from 0 to 137
- skip_gain: float32 [64], replicated, may hold values from 0.5 to 2
- gate_gain: float32 [4096], P('chan'), may hold values from 0.25 to 1.75
- w_out: bfloat16 [4096, 2048], P('chan'), may hold values from -0.125 to 0.125
- doc_starts: int32 [4], replicated, may hold values from 0 to 3328, as said below
Outputs:
- layer_out: bfloat16 [4096, 4096], P('seq', 'chan')
The draws below stay inside these ranges and needn't reach their ends.
Inputs may be any that keep to these rules, and one draw needn't show every extreme that they name: doc_starts[0] is 0 and the offsets rise strictly; document k runs from doc_starts[k] up to the next offset or the window's end.
All inputs are finite; a program needn't handle non-finite values.
Results may differ from the reference program's by a relative error of at most 0.013.
Values may be sent and summed in bfloat16 or wider, within the bound.
No kernel may reach another device: no remote copies, remote signals or barrier semaphores. Data moves between devices by JAX's collectives and lax.ppermute only.
A program may use at most 128 MiB of HBM per device.

```python
import math
import jax
import jax.numpy as jnp
from jax import lax

D = 4096
HALF = 2048
INNER = 4096
HEAD_DIM = 64
STATE = 128
STRETCH = 256
HEADS = 64
SEQ_LEN = 4096
DOCS = 4


def draw_decay_total(key, part):
    key_slow, key_fast, key_pick = jax.random.split(jax.random.fold_in(key, 17), 3)
    slow_rates = jnp.exp(jax.random.uniform(key_slow, (HEADS,), jnp.float32, math.log(0.05), math.log(2.0)))
    fast_rates = jnp.exp(jax.random.uniform(key_fast, (HEADS,), jnp.float32, math.log(SEQ_LEN / 50.0), math.log(SEQ_LEN / 30.0)))
    share_slow = 0.5
    chosen = jax.random.uniform(key_pick, (HEADS,), jnp.float32) < share_slow
    return jnp.where(chosen, slow_rates, fast_rates).astype(jnp.float32)


def draw_doc_starts(key, part):
    doc_span = SEQ_LEN // DOCS
    jitter = SEQ_LEN // (4 * DOCS)
    offsets = jax.random.randint(jax.random.fold_in(key, 29), (DOCS,), -jitter, jitter + 1)
    doc_index = jnp.arange(DOCS, dtype=jnp.int32)
    offsets = jnp.where(doc_index == DOCS - 1, jitter, offsets)
    return jnp.where(doc_index == 0, 0, doc_index * doc_span + offsets).astype(jnp.int32)


def spiked(entries, own_key, source, target, blocks, factor):
    def block_of(axis_at):
        return (jnp.arange(entries.shape[axis_at]) // (entries.shape[axis_at] // blocks)).reshape((-1,) + (1,) * (entries.ndim - 1 - axis_at))

    near = jax.random.permutation(own_key, blocks)[block_of(target)]
    second = (block_of(target) + blocks // 2) % blocks
    return jnp.where((block_of(source) == near) | (block_of(source) == second), factor * entries, entries)


def levels(key, shape, cuts, least, largest):
    level = 1.0
    for position, blocks in cuts:
        steps = jax.random.uniform(jax.random.fold_in(jax.random.fold_in(key, 6), position), (blocks,), jnp.float32, least / len(cuts), largest / len(cuts))
        level = level * jnp.repeat(jnp.exp(steps), shape[position] // blocks).reshape((-1,) + (1,) * (len(shape) - 1 - position))
    return level


def centred(rng, dims, width, limit, cuts=(), held_as=jnp.bfloat16):
    result = width * jax.random.normal(rng, dims, jnp.float32)
    if cuts:
        result = result * levels(rng, dims, cuts, -0.22, 0.18)
    return jnp.clip(result, -limit, limit).astype(held_as)


def heavy_noise(stream_key, extent, scale, reach, cuts, heavy, kind=jnp.bfloat16):
    drawn = scale * jax.random.normal(stream_key, extent, jnp.float32)
    if cuts:
        drawn = drawn * levels(stream_key, extent, cuts, -0.22, 0.18)
    return jnp.clip(spiked(drawn, jax.random.fold_in(stream_key, 3), *heavy), -reach, reach).astype(kind)


def setup_inputs(seed: int = 0) -> dict:
    keys = jax.random.split(jax.random.key(seed), 12)
    return {
        "hidden": centred(keys[0], (SEQ_LEN, D), 1.0, 6.0, ((0, 8), (1, 4))),
        "norm_gain": jnp.clip(1.0 + 0.15 * jax.random.normal(keys[1], (HALF,), jnp.float32), 0.25, 1.75),
        "w_values": centred(keys[2], (HALF, INNER), HALF ** -0.5, 0.125, ((1, 4),)),
        "w_gates": centred(keys[3], (HALF, INNER), HALF ** -0.5, 0.125, ((1, 4),)),
        "w_control": centred(keys[4], (HALF, 2 * STATE + HEADS), (HALF * 8) ** -0.5, 0.046875),
        "dt_bias": jnp.clip(jax.random.uniform(keys[5], (HEADS,), jnp.float32, -1.0, 1.0), -1.0, 1.0),
        "decay_total": draw_decay_total(jax.random.fold_in(keys[11], 71), 0),
        "skip_gain": jnp.clip(jax.random.uniform(keys[7], (HEADS,), jnp.float32, 0.5, 2.0), 0.5, 2.0),
        "gate_gain": jnp.clip(1.0 + 0.15 * jax.random.normal(keys[8], (INNER,), jnp.float32), 0.25, 1.75),
        "w_out": heavy_noise(keys[9], (INNER, HALF), INNER ** -0.5, 0.125, ((0, 4),), (0, 1, 4, 2.0)),
        "doc_starts": draw_doc_starts(jax.random.fold_in(keys[11], 71), 0),
    }


norm_eps = 1e-05
highest = lax.Precision.HIGHEST

def segment_ids(positions, doc_starts):
    return (lax.optimization_barrier(jnp.sum((positions[:, None] >= doc_starts[None, :]).astype(jnp.int32), axis=1)) - 1).astype(jnp.int32)

def combine_stretches(earlier, latter):
    return (earlier[0] * latter[0], latter[0][..., None, :, None] * earlier[1] + latter[1])

def stretch_scan(inputs, log_decay, step_size, b_in, c_out, segment, seg_before):
    total_len, groups, head_width = inputs.shape
    blocks = total_len // STRETCH
    weighted = (inputs * step_size[:, :, None]).reshape(blocks, STRETCH, groups, head_width)
    running = jnp.cumsum(log_decay.reshape(blocks, STRETCH, groups), axis=1)
    stretch_total = running[:, -1]
    b_blocks = b_in.reshape(blocks, STRETCH, -1)
    c_blocks = c_out.reshape(blocks, STRETCH, -1)
    seg_blocks = segment.reshape(blocks, STRETCH)
    scores = jnp.einsum('kqn,ksn->kqs', c_blocks.astype(jnp.float32), b_blocks.astype(jnp.float32))
    by_group = jnp.transpose(running, (0, 2, 1))
    log_gaps = by_group[:, :, :, None] - by_group[:, :, None, :]
    index_rows = jnp.arange(STRETCH, dtype=jnp.int32)
    allowed = (index_rows[:, None] >= index_rows[None, :])[None] & (seg_blocks[:, :, None] == seg_blocks[:, None, :])
    decay_mask = jnp.exp(jnp.where(allowed[:, None], log_gaps, -jnp.inf))
    within = jnp.einsum('kgts,ksgw->ktgw', decay_mask * scores[:, None], weighted, precision=highest)
    toward_end = jnp.exp(stretch_total[:, None, :] - running) * (seg_blocks == seg_blocks[:, -1:]).astype(jnp.float32)[:, :, None]
    stretch_states = jnp.einsum('ksn,ksgw->kngw', b_blocks.astype(jnp.float32), weighted * toward_end[..., None], precision=highest)
    seg_prior = jnp.concatenate([jnp.reshape(seg_before, (1,)).astype(jnp.int32), seg_blocks[:-1, -1]])
    stretch_keep = jnp.exp(stretch_total) * (seg_blocks[:, -1] == seg_prior).astype(jnp.float32)[:, None]
    keep_incl, state_incl = lax.associative_scan(combine_stretches, (stretch_keep, stretch_states))
    state_prior = jnp.concatenate([jnp.zeros_like(stretch_states[:1]), state_incl[:-1]])
    reach_factor = jnp.exp(running) * (seg_blocks == seg_prior[:, None]).astype(jnp.float32)[:, :, None]
    carried = jnp.einsum('kqn,kngw->kqgw', c_blocks.astype(jnp.float32), state_prior, precision=highest) * reach_factor[..., None]
    return ((within + carried).reshape(total_len, groups, head_width), keep_incl[-1], state_incl[-1])

def strand_scan(values, control, segment, dt_bias, decay_total, skip_gain):
    length = values.shape[0]
    b_in = control[:, :STATE]
    c_out = control[:, STATE:2 * STATE]
    step_size = jax.nn.softplus(control[:, 2 * STATE:].astype(jnp.float32) + dt_bias)
    log_decay = -(decay_total / SEQ_LEN) * step_size
    group_size = math.gcd(HEADS, 8)
    group_count = HEADS // group_size
    inputs = values.astype(jnp.float32).reshape(length, group_count, group_size, HEAD_DIM).transpose(1, 0, 2, 3)
    decay_groups = log_decay.reshape(length, group_count, group_size).transpose(1, 0, 2)
    step_groups = step_size.reshape(length, group_count, group_size).transpose(1, 0, 2)
    skip_groups = skip_gain.reshape(group_count, group_size)
    no_segment = jnp.int32(-1)

    def scan_group(operands):
        part_in, part_decay, part_step, part_skip = operands
        forward = stretch_scan(part_in, part_decay, part_step, b_in, c_out, segment, no_segment)[0]
        backward = stretch_scan(part_in[::-1], part_decay[::-1], part_step[::-1], b_in[::-1], c_out[::-1], segment[::-1], no_segment)[0][::-1]
        direct = part_skip[None, :, None] * part_in
        return jnp.stack([forward + direct, backward + direct])
    scanned = lax.map(scan_group, (inputs, decay_groups, step_groups, skip_groups))
    return scanned.transpose(1, 2, 0, 3, 4).reshape(2, length, INNER).astype(jnp.bfloat16)

def reference(hidden, norm_gain, w_values, w_gates, w_control, dt_bias, decay_total, skip_gain, gate_gain, w_out, doc_starts):
    strands = jnp.stack([hidden[:, :HALF], hidden[:, HALF:][:, ::-1]])
    widened = strands.astype(jnp.float32)
    normed = (widened * lax.rsqrt(lax.optimization_barrier(jnp.mean(widened * widened, axis=-1, keepdims=True)) + norm_eps) * norm_gain).astype(jnp.bfloat16)
    normed_wide = normed.astype(jnp.float32)
    values = jnp.einsum('sth,he->ste', normed_wide, w_values.astype(jnp.float32)).astype(jnp.bfloat16)
    gates = jnp.einsum('sth,he->ste', normed_wide, w_gates.astype(jnp.float32)).astype(jnp.bfloat16)
    control = jnp.einsum('sth,he->ste', normed_wide, w_control.astype(jnp.float32)).astype(jnp.bfloat16)
    segment = segment_ids(jnp.arange(SEQ_LEN, dtype=jnp.int32), doc_starts)
    results = []
    for strand in range(2):
        scanned = strand_scan(values[strand], control[strand], segment, dt_bias, decay_total, skip_gain)
        gate_wide = gates[strand].astype(jnp.float32)
        activated = gate_wide * jax.nn.sigmoid(gate_wide)
        gated_values = scanned.astype(jnp.float32) * activated[None]
        scaled = gated_values * lax.rsqrt(lax.optimization_barrier(jnp.mean(gated_values * gated_values, axis=-1, keepdims=True)) + norm_eps) * gate_gain
        combined = (scaled[0] + scaled[1]).astype(jnp.bfloat16)
        results.append(jnp.dot(combined, w_out, preferred_element_type=jnp.float32))
    layer_out = jnp.concatenate([results[0], results[1][:, ::-1]], axis=1).astype(jnp.bfloat16)
    return layer_out
```

```python
import functools

import jax
import jax.numpy as jnp
from jax import lax
from jax.experimental import pallas as pl
from jax.experimental.pallas import tpu as pltpu
from jax.sharding import PartitionSpec as P

HEAD_DIM = 64
STATE = 128
CHUNK = 128
LANES = 128
REV = 256
KEEP_ROWS = 16

norm_eps = 1e-05
highest = lax.Precision.HIGHEST
f32 = jnp.float32
bf16 = jnp.bfloat16


def mm(a, b):
    return jnp.dot(a, b, preferred_element_type=f32)


def mm_nt(a, b):
    return lax.dot_general(a, b, (((1,), (1,)), ((), ())), preferred_element_type=f32)


def mm_tn(a, b):
    return lax.dot_general(a, b, (((0,), (0,)), ((), ())), preferred_element_type=f32)


def iota(shape, dim):
    return lax.broadcasted_iota(jnp.int32, shape, dim)


def exchange_matrix(mirror):
    row, col = iota((REV, REV), 0), iota((REV, REV), 1)
    return (row == jnp.where(mirror == 1, REV - 1 - col, col)).astype(f32).astype(bf16)


def segment_of(position, starts_ref):
    total = jnp.zeros_like(position)
    for k in range(starts_ref.shape[0]):
        total = total + (position >= starts_ref[k]).astype(jnp.int32)
    return total


def expander(width):
    row, col = iota((2 * LANES, width), 0), iota((2 * LANES, width), 1)
    return ((row % LANES) == (col // HEAD_DIM)).astype(f32).astype(bf16)


def expand(w, spread):
    high = w.astype(bf16)
    low = (w - high.astype(f32)).astype(bf16)
    return mm(jnp.concatenate([high, low], axis=1), spread)


def full(shape):
    return pl.BlockSpec(shape, lambda *_: (0,) * len(shape))


SMEM = pl.BlockSpec(memory_space=pltpu.SMEM)


def norm_project_kernel(pieces, mirror_ref, *refs):
    xs = refs[:pieces]
    gain_ref, wv_ref, wc_ref, normed_ref, values_ref, control_ref, scr = refs[pieces:]
    half = normed_ref.shape[1]
    blocks = half // REV

    @pl.when(pl.program_id(0) == 0)
    def _():
        mirror = mirror_ref[0]
        swap = exchange_matrix(mirror)
        squares = jnp.zeros((normed_ref.shape[0], 1), f32)
        at = 0
        for x_ref in xs:
            for q in range(x_ref.shape[1] // REV):
                xb = x_ref[:, q * REV : (q + 1) * REV]
                wide = xb.astype(f32)
                squares = squares + jnp.sum(wide * wide, axis=1, keepdims=True)
                scr[jnp.where(mirror == 1, blocks - 1 - at, at)] = mm(xb, swap).astype(bf16)
                at += 1
        scale = lax.rsqrt(squares / half + norm_eps)
        for q in range(blocks):
            cols = slice(q * REV, (q + 1) * REV)
            normed_ref[:, cols] = (scr[q].astype(f32) * scale * gain_ref[:, cols]).astype(bf16)
        control_ref[...] = mm(normed_ref[...], wc_ref[...]).astype(bf16)

    values_ref[...] = mm(normed_ref[...], wv_ref[...]).astype(bf16)


def norm_project(xs, mirror, gain, w_values, w_control):
    tokens = xs[0].shape[0]
    half, cols = w_values.shape
    tile = min(256, cols)
    return pl.pallas_call(
        functools.partial(norm_project_kernel, len(xs)),
        grid=(cols // tile,),
        in_specs=[SMEM]
        + [full(x.shape) for x in xs]
        + [full(gain.shape), pl.BlockSpec((half, tile), lambda j: (0, j)), full(w_control.shape)],
        out_specs=[
            full((tokens, half)),
            pl.BlockSpec((tokens, tile), lambda j: (0, j)),
            full((tokens, w_control.shape[1])),
        ],
        out_shape=[
            jax.ShapeDtypeStruct((tokens, half), bf16),
            jax.ShapeDtypeStruct((tokens, cols), bf16),
            jax.ShapeDtypeStruct((tokens, w_control.shape[1]), bf16),
        ],
        scratch_shapes=[pltpu.VMEM((half // REV, tokens, REV), bf16)],
        name="norm_project",
    )(mirror, *xs, gain, w_values, w_control)


def states_kernel(
    starts_ref, base_ref, control_ref, values_ref, par_ref,
    total_ref, pre_ref, cola_ref, colb_ref, rowf_ref, rowb_ref, reach_ref,
):
    tokens, cols = values_ref.shape
    chunks = tokens // CHUNK
    heads = cols // HEAD_DIM
    base = base_ref[0]
    spread = expander(cols)
    row, col = iota((CHUNK, CHUNK), 0), iota((CHUNK, CHUNK), 1)
    tri = (row >= col).astype(f32)
    seg_at = lambda offset: segment_of(base + jnp.full((1, 1), offset, jnp.int32), starts_ref)
    pieces = []
    for k in range(chunks):
        rows = slice(k * CHUNK, (k + 1) * CHUNK)
        raw = control_ref[rows, 2 * STATE :].astype(f32) + par_ref[0:1, :]
        step = jnp.maximum(raw, 0.0) + jnp.log1p(jnp.exp(-jnp.abs(raw)))
        log_step = jnp.log(step)
        log_rate = -par_ref[1:2, :] * step
        cum = jnp.dot(tri, log_rate, precision=highest, preferred_element_type=f32)
        before = cum - log_rate
        whole = cum[CHUNK - 1 : CHUNK, :]
        cola_ref[rows, :] = cum
        colb_ref[rows, :] = before
        rowf_ref[k] = jnp.transpose(cum - log_step)[:heads]
        rowb_ref[k] = jnp.transpose(before + log_step)[:heads]
        seg = segment_of(base + k * CHUNK + iota((CHUNK, 1), 0), starts_ref)
        first, last = seg_at(k * CHUNK), seg_at((k + 1) * CHUNK - 1)
        prior, after = seg_at(k * CHUNK - 1), seg_at((k + 1) * CHUNK)
        w_f = jnp.where(seg == last, step * jnp.exp(whole - cum), 0.0)
        w_b = jnp.where(seg == first, step * jnp.exp(before), 0.0)
        b_in = control_ref[rows, :STATE]
        wide = values_ref[rows, :].astype(f32)
        add_f = mm_tn(b_in, (wide * expand(w_f, spread)).astype(bf16))
        add_b = mm_tn(b_in, (wide * expand(w_b, spread)).astype(bf16))
        keep = jnp.exp(whole)
        keep_f = jnp.where(prior == last, keep, 0.0)
        keep_b = jnp.where(first == after, keep, 0.0)
        pieces.append((seg, cum, before, whole, add_f, add_b, keep_f, keep_b))
    lift = lambda w: expand(jnp.broadcast_to(w, (8, LANES)), spread)[0:1]
    for d, order in enumerate((range(chunks), range(chunks - 1, -1, -1))):
        state = jnp.zeros((STATE, cols), f32)
        keep_all = jnp.ones((1, LANES), f32)
        shift = jnp.zeros((1, LANES), f32)
        edge = seg_at(-1) if d == 0 else seg_at(tokens)
        for k in order:
            seg, cum, before, whole, add_f, add_b, keep_f, keep_b = pieces[k]
            pre_ref[d, k] = state.astype(bf16)
            add, keep = (add_f, keep_f) if d == 0 else (add_b, keep_b)
            inner = cum if d == 0 else whole - before
            reach_ref[d, k * CHUNK : (k + 1) * CHUNK, :] = jnp.where(
                seg == edge, jnp.exp(inner + shift), 0.0
            )
            state = lift(keep) * state + add
            keep_all = keep_all * keep
            shift = shift + whole
        total_ref[d, :STATE] = state.astype(bf16)
        total_ref[d, STATE:] = jnp.broadcast_to(lift(keep_all), (KEEP_ROWS, cols)).astype(bf16)


def chunk_states(starts, base, control, values, par):
    tokens, cols = values.shape
    chunks, heads = tokens // CHUNK, cols // HEAD_DIM
    shapes = [
        ((2, STATE + KEEP_ROWS, cols), bf16),
        ((2, chunks, STATE, cols), bf16),
        ((tokens, LANES), f32),
        ((tokens, LANES), f32),
        ((chunks, heads, CHUNK), f32),
        ((chunks, heads, CHUNK), f32),
        ((2, tokens, LANES), f32),
    ]
    return pl.pallas_call(
        states_kernel,
        grid=(1,),
        in_specs=[SMEM, SMEM, full(control.shape), full(values.shape), full(par.shape)],
        out_specs=[full(s) for s, _ in shapes],
        out_shape=[jax.ShapeDtypeStruct(s, t) for s, t in shapes],
        name="chunk_states",
    )(starts, base, control, values, par)


def within_kernel(
    starts_ref, base_ref, control_ref, values_ref, skip_ref,
    pre_ref, cola_ref, colb_ref, rowf_ref, rowb_ref, out_ref,
):
    cols = values_ref.shape[1]
    k = pl.program_id(0)
    start = base_ref[0] + k * CHUNK
    spread = expander(cols)
    row, col = iota((CHUNK, CHUNK), 0), iota((CHUNK, CHUNK), 1)
    low_lanes = iota((CHUNK, LANES), 1) < HEAD_DIM
    b_in, c_out = control_ref[:, :STATE], control_ref[:, STATE : 2 * STATE]
    seg_col = segment_of(start + iota((CHUNK, 1), 0), starts_ref)
    seg_row = segment_of(start + iota((1, CHUNK), 1), starts_ref)
    prior = segment_of(jnp.full((1, 1), start - 1, jnp.int32), starts_ref)
    after = segment_of(jnp.full((1, 1), start + CHUNK, jnp.int32), starts_ref)
    same = seg_col == seg_row
    lower = row >= col
    scores = mm_nt(c_out, b_in)
    scores_f = jnp.where(lower & same, scores, 0.0)
    scores_b = jnp.where((row <= col) & same, scores, 0.0)
    cum, before = cola_ref[...], colb_ref[...]
    whole = cum[CHUNK - 1 : CHUNK, :]
    far_f = expand(jnp.where(seg_col == prior, jnp.exp(cum), 0.0), spread)
    far_b = expand(jnp.where(seg_col == after, jnp.exp(whole - before), 0.0), spread)
    carry_f = mm(c_out, pre_ref[0, 0]) * far_f
    carry_b = mm(c_out, pre_ref[1, 0]) * far_b
    per_tile = LANES // HEAD_DIM
    for pair in range(cols // LANES):
        lanes = slice(pair * LANES, (pair + 1) * LANES)
        value = values_ref[:, lanes]
        left_f, left_b = [], []
        for h in range(pair * per_tile, (pair + 1) * per_tile):
            gap = jnp.where(
                lower,
                cum[:, h : h + 1] - rowf_ref[0, h : h + 1, :],
                rowb_ref[0, h : h + 1, :] - before[:, h : h + 1],
            )
            weight = jnp.exp(gap)
            left_f.append((weight * scores_f).astype(bf16))
            left_b.append((weight * scores_b).astype(bf16))
        left = jnp.concatenate(
            [jnp.concatenate(left_f, axis=1), jnp.concatenate(left_b, axis=1)], axis=0
        )
        zero = jnp.zeros_like(value)
        right = jnp.concatenate(
            [jnp.where(low_lanes, value, zero), jnp.where(low_lanes, zero, value)], axis=0
        )
        near = mm(left, right)
        direct = value.astype(f32) * skip_ref[:, lanes]
        out_ref[0, :, lanes] = near[:CHUNK] + carry_f[:, lanes] + direct
        out_ref[1, :, lanes] = near[CHUNK:] + carry_b[:, lanes] + direct


def within(starts, base, control, values, skip_row, pre, cola, colb, rowf, rowb):
    tokens, cols = values.shape
    chunks, heads = tokens // CHUNK, cols // HEAD_DIM
    rows = lambda width: pl.BlockSpec((CHUNK, width), lambda k: (k, 0))
    return pl.pallas_call(
        within_kernel,
        grid=(chunks,),
        in_specs=[
            SMEM, SMEM,
            rows(control.shape[1]), rows(cols), full(skip_row.shape),
            pl.BlockSpec((2, 1, STATE, cols), lambda k: (0, k, 0, 0)),
            rows(LANES), rows(LANES),
            pl.BlockSpec((1, heads, CHUNK), lambda k: (k, 0, 0)),
            pl.BlockSpec((1, heads, CHUNK), lambda k: (k, 0, 0)),
        ],
        out_specs=pl.BlockSpec((2, CHUNK, cols), lambda k: (0, k, 0)),
        out_shape=jax.ShapeDtypeStruct((2, tokens, cols), f32),
        name="within_chunk",
    )(starts, base, control, values, skip_row, pre, cola, colb, rowf, rowb)


def gate_kernel(control_ref, near_ref, into_ref, reach_ref, gates_ref, out_ref, squares_ref):
    cols = gates_ref.shape[1]
    spread = expander(cols)
    c_out = control_ref[:, STATE : 2 * STATE]
    gate = gates_ref[...].astype(f32)
    active = gate * jax.nn.sigmoid(gate)
    lane = iota((CHUNK, LANES), 1)
    squares = jnp.zeros((CHUNK, LANES), f32)
    for d in range(2):
        carry = mm(c_out, into_ref[d]) * expand(reach_ref[d], spread)
        y = (near_ref[d] + carry).astype(bf16).astype(f32)
        v = y * active
        squares = jnp.where(lane == d, jnp.sum(v * v, axis=1, keepdims=True), squares)
        out_ref[d] = v.astype(bf16)
    squares_ref[...] = jnp.transpose(squares)[:8]


def carry_gate(control, near, into, reach, gates):
    tokens, cols = gates.shape
    rows = lambda width: pl.BlockSpec((CHUNK, width), lambda k: (k, 0))
    both = lambda width: pl.BlockSpec((2, CHUNK, width), lambda k: (0, k, 0))
    return pl.pallas_call(
        gate_kernel,
        grid=(tokens // CHUNK,),
        in_specs=[rows(control.shape[1]), both(cols), full(into.shape), both(LANES), rows(cols)],
        out_specs=[both(cols), pl.BlockSpec((8, CHUNK), lambda k: (0, k))],
        out_shape=[
            jax.ShapeDtypeStruct((2, tokens, cols), bf16),
            jax.ShapeDtypeStruct((8, tokens), f32),
        ],
        name="carry_gate",
    )(control, near, into, reach, gates)


def output_kernel(inner, sums, mirror_ref, gated_ref, *refs):
    squares_refs = refs[:sums]
    gain_ref, w_ref, out_ref = refs[sums:]
    squares = squares_refs[0][...]
    for other in squares_refs[1:]:
        squares = squares + other[...]
    scale = lax.rsqrt(squares / inner + norm_eps)
    scale = jnp.transpose(jnp.concatenate([scale, jnp.zeros((CHUNK - 8, CHUNK), f32)], axis=0))
    gain = gain_ref[...]
    combined = (
        gated_ref[0].astype(f32) * scale[:, 0:1] * gain
        + gated_ref[1].astype(f32) * scale[:, 1:2] * gain
    ).astype(bf16)
    product = mm(combined, w_ref[...]).astype(bf16)
    width = product.shape[1]
    blocks = width // REV

    @pl.when(mirror_ref[0] == 0)
    def _():
        out_ref[...] = product

    @pl.when(mirror_ref[0] == 1)
    def _():
        swap = exchange_matrix(jnp.int32(1))
        for q in range(blocks):
            back = blocks - 1 - q
            out_ref[:, back * REV : (back + 1) * REV] = mm(
                product[:, q * REV : (q + 1) * REV], swap
            ).astype(bf16)


def output_project(inner, mirror, gated, squares, gain_row, w_out):
    _, tokens, cols = gated.shape
    width = w_out.shape[1]
    return pl.pallas_call(
        functools.partial(output_kernel, inner, len(squares)),
        grid=(tokens // CHUNK,),
        in_specs=[SMEM, pl.BlockSpec((2, CHUNK, cols), lambda k: (0, k, 0))]
        + [pl.BlockSpec((8, CHUNK), lambda k: (0, k)) for _ in squares]
        + [full(gain_row.shape), full(w_out.shape)],
        out_specs=pl.BlockSpec((CHUNK, width), lambda k: (k, 0)),
        out_shape=jax.ShapeDtypeStruct((tokens, width), bf16),
        name="output_project",
    )(mirror, gated, *squares, gain_row, w_out)


def incoming_states(total):
    count = lax.axis_size("seq")
    place = lax.axis_index("seq")
    group = total
    into = [jnp.zeros(total.shape[1:], f32)] * 2
    into_keep = [jnp.ones((1, total.shape[2]), f32)] * 2
    stride = 1
    while stride < count:
        got = lax.ppermute(group, "seq", [(i, i ^ stride) for i in range(count)]).astype(f32)
        mine = group.astype(f32)
        upper = (place // stride) % 2 == 1
        merged = []
        for d in range(2):
            after_got = upper if d == 0 else jnp.logical_not(upper)
            got_keep, my_keep = got[d, STATE : STATE + 1], mine[d, STATE : STATE + 1]
            into[d] = jnp.where(after_got, into_keep[d] * got[d] + into[d], into[d])
            into_keep[d] = jnp.where(after_got, into_keep[d] * got_keep, into_keep[d])
            late, early = jnp.where(after_got, mine[d], got[d]), jnp.where(after_got, got[d], mine[d])
            late_keep = jnp.where(after_got, my_keep, got_keep)
            states = late_keep * early[:STATE] + late[:STATE]
            merged.append(jnp.concatenate([states, early[STATE:] * late[STATE:]], axis=0))
        group = jnp.stack(merged).astype(bf16)
        stride *= 2
    return jnp.stack([into[0][:STATE], into[1][:STATE]]).astype(bf16)


def chan_parts(part):
    count = lax.axis_size("chan")
    others = [
        lax.ppermute(part, "chan", [(i, (i + k) % count) for i in range(count)])
        for k in range(1, count)
    ]
    return [part] + others


def local(
    hidden, norm_gain, w_values, w_gates, w_control, dt_bias, decay_total, skip_gain, gate_gain,
    w_out, doc_starts,
):
    seq_count, chan_count = lax.axis_size("seq"), lax.axis_size("chan")
    seq_rank, chan_rank = lax.axis_index("seq"), lax.axis_index("chan")
    tokens = hidden.shape[0]
    half = norm_gain.shape[0]
    cols = w_values.shape[1]
    heads = cols // HEAD_DIM
    mine = lambda a, axis: lax.dynamic_slice_in_dim(a, chan_rank * heads, heads, axis)
    lanes = lambda a: jnp.pad(a, ((0, 0), (0, LANES - heads)))
    w_steps = lanes(mine(w_control[:, 2 * STATE :], 1))
    w_small = jnp.concatenate([w_control[:, : 2 * STATE], w_steps], axis=1)
    par = lanes(jnp.stack([mine(dt_bias, 0), mine(decay_total, 0) / (tokens * seq_count)]))
    par = jnp.pad(par, ((0, 6), (0, 0)))
    skip_row = jnp.repeat(mine(skip_gain, 0), HEAD_DIM)[None]
    gain_row, gate_row = norm_gain[None], gate_gain[None]
    base = jnp.reshape(seq_rank * tokens, (1,)).astype(jnp.int32)
    whole = lax.all_gather(hidden, "chan", axis=1, tiled=True)
    parts = []
    for strand in range(2):
        mirror = jnp.full((1,), strand, jnp.int32)
        x = whole[:, strand * half : (strand + 1) * half]
        normed, values, control = norm_project([x], mirror, gain_row, w_values, w_small)
        total, pre, cola, colb, rowf, rowb, reach = chunk_states(
            doc_starts, base, control, values, par
        )
        into = incoming_states(total)
        gates = mm(normed, w_gates).astype(bf16)
        near = within(doc_starts, base, control, values, skip_row, pre, cola, colb, rowf, rowb)
        gated, squares = carry_gate(control, near, into, reach, gates)
        parts.append(
            output_project(
                cols * chan_count, mirror, gated, chan_parts(squares), gate_row, w_out
            )
        )
    partial_value = jnp.concatenate(parts, axis=1)
    return lax.psum_scatter(partial_value, "chan", scatter_dimension=1, tiled=True)


def solution(mesh):
    in_specs = (
        P("seq", "chan"), P(), P(None, "chan"), P(None, "chan"), P(), P(), P(), P(), P("chan"),
        P("chan", None), P(),
    )
    return jax.shard_map(
        local, mesh=mesh, in_specs=in_specs, out_specs=P("seq", "chan"), check_vma=False
    )
```

```python
import functools

import jax
import jax.numpy as jnp
from jax import lax
from jax.experimental import pallas as pl
from jax.experimental.pallas import tpu as pltpu
from jax.sharding import PartitionSpec as P


HEAD_DIM = 64
STATE = 128
CHUNK = 128
LANES = 128
REV = 256
KEEP_ROWS = 16
PIECES = 2


norm_eps = 1e-05
highest = lax.Precision.HIGHEST
f32 = jnp.float32
bf16 = jnp.bfloat16


def mm(a, b):
    return jnp.dot(a, b, preferred_element_type=f32)


def mm_nt(a, b):
    return lax.dot_general(a, b, (((1,), (1,)), ((), ())), preferred_element_type=f32)


def mm_tn(a, b):
    return lax.dot_general(a, b, (((0,), (0,)), ((), ())), preferred_element_type=f32)


def iota(shape, dim):
    return lax.broadcasted_iota(jnp.int32, shape, dim)


def exchange_matrix(mirror):
    row, col = iota((REV, REV), 0), iota((REV, REV), 1)
    return (row == jnp.where(mirror == 1, REV - 1 - col, col)).astype(f32).astype(bf16)


def segment_of(position, starts_ref):
    total = jnp.zeros_like(position)
    for k in range(starts_ref.shape[0]):
        total = total + (position >= starts_ref[k]).astype(jnp.int32)
    return total


def expander(width):
    row, col = iota((2 * LANES, width), 0), iota((2 * LANES, width), 1)
    return ((row % LANES) == (col // HEAD_DIM)).astype(f32).astype(bf16)


def expand(w, spread):
    high = w.astype(bf16)
    low = (w - high.astype(f32)).astype(bf16)
    return mm(jnp.concatenate([high, low], axis=1), spread)


def full(shape):
    return pl.BlockSpec(shape, lambda *_: (0,) * len(shape))


SMEM = pl.BlockSpec(memory_space=pltpu.SMEM)


def norm_project_kernel(routes, rank_ref, mirror_ref, *refs):
    slots, pieces = len(routes[0]), len(routes[0][0])
    xs = refs[: 1 + max(at for by_slot in routes for row in by_slot for at in row)]
    gain_ref, wa_ref, wb_ref, wc_ref, normed_ref, values_ref, control_ref, scr, held, sems = refs[
        len(xs) :
    ]
    half = normed_ref.shape[1]
    blocks = half // REV
    _, tokens, width = held.shape
    rows = tokens // pieces

    @pl.when(pl.program_id(0) == 0)
    def _():
        rank, mirror = rank_ref[0], mirror_ref[0]
        target = lambda j, p: held.at[j, pl.ds(p * rows, rows), :]
        for r, by_slot in enumerate(routes):

            @pl.when(rank == r)
            def _():
                for j in range(slots):
                    for p in range(pieces):
                        pltpu.make_async_copy(
                            xs[by_slot[j][p]], target(j, p), sems.at[j, p]
                        ).start()

        swap = exchange_matrix(mirror)
        squares = jnp.zeros((tokens, 1), f32)
        at = 0
        for j in range(slots):
            for p in range(pieces):
                pltpu.make_async_copy(xs[0], target(j, p), sems.at[j, p]).wait()
            for q in range(width // REV):
                xb = held[j, :, q * REV : (q + 1) * REV]
                wide = xb.astype(f32)
                squares = squares + jnp.sum(wide * wide, axis=1, keepdims=True)
                scr[jnp.where(mirror == 1, blocks - 1 - at, at)] = mm(xb, swap).astype(bf16)
                at += 1
        scale = lax.rsqrt(squares / half + norm_eps)
        for q in range(blocks):
            cols = slice(q * REV, (q + 1) * REV)
            normed_ref[:, cols] = (scr[q].astype(f32) * scale * gain_ref[:, cols]).astype(bf16)
        control_ref[...] = mm(normed_ref[...], wc_ref[...]).astype(bf16)

    two_weights(normed_ref, wa_ref, wb_ref, values_ref)


def two_weights(x_ref, wa_ref, wb_ref, out_ref):
    first = pl.program_id(0) < pl.num_programs(0) // 2

    @pl.when(first)
    def _():
        out_ref[...] = mm(x_ref[...], wa_ref[...]).astype(bf16)

    @pl.when(jnp.logical_not(first))
    def _():
        out_ref[...] = mm(x_ref[...], wb_ref[...]).astype(bf16)


def weight_specs(half, tile, steps):
    return [
        pl.BlockSpec((half, tile), lambda j: (0, jnp.minimum(j, steps - 1))),
        pl.BlockSpec((half, tile), lambda j: (0, jnp.maximum(j - steps, 0))),
    ]


def project(x, weights):
    tokens, half = x.shape
    cols = weights[0].shape[1]
    tile = min(256, cols)
    steps = cols // tile
    return pl.pallas_call(
        two_weights,
        grid=(2 * steps,),
        in_specs=[full(x.shape)] + weight_specs(half, tile, steps),
        out_specs=pl.BlockSpec((tokens, tile), lambda j: (0, j)),
        out_shape=jax.ShapeDtypeStruct((tokens, 2 * cols), bf16),
        name="project",
    )(x, *weights)


def norm_project(routes, xs, rank, mirror, gain, weights, w_control):
    slots, pieces = len(routes[0]), len(routes[0][0])
    tokens = xs[0].shape[0] * pieces
    half, cols = weights[0].shape
    tile = min(256, cols)
    steps = cols // tile
    return pl.pallas_call(
        functools.partial(norm_project_kernel, routes),
        grid=(2 * steps,),
        in_specs=[SMEM, SMEM]
        + [pl.BlockSpec(memory_space=pl.ANY) for x in xs]
        + [full(gain.shape)]
        + weight_specs(half, tile, steps)
        + [full(w_control.shape)],
        out_specs=[
            full((tokens, half)),
            pl.BlockSpec((tokens, tile), lambda j: (0, j)),
            full((tokens, w_control.shape[1])),
        ],
        out_shape=[
            jax.ShapeDtypeStruct((tokens, half), bf16),
            jax.ShapeDtypeStruct((tokens, 2 * cols), bf16),
            jax.ShapeDtypeStruct((tokens, w_control.shape[1]), bf16),
        ],
        scratch_shapes=[
            pltpu.VMEM((half // REV, tokens, REV), bf16),
            pltpu.VMEM((slots, tokens, half // slots), bf16),
            pltpu.SemaphoreType.DMA((slots, pieces)),
        ],
        name="norm_project",
    )(rank, mirror, *xs, gain, *weights, w_control)


def states_kernel(
    starts_ref, base_ref, control_ref, values_ref, par_ref,
    total_ref, pre_ref, cola_ref, colb_ref, rowf_ref, rowb_ref, reach_ref,
):
    tokens, cols = values_ref.shape
    chunks = tokens // CHUNK
    heads = cols // HEAD_DIM
    base = base_ref[0]
    spread = expander(cols)
    row, col = iota((CHUNK, CHUNK), 0), iota((CHUNK, CHUNK), 1)
    tri = (row >= col).astype(f32)
    seg_at = lambda offset: segment_of(base + jnp.full((1, 1), offset, jnp.int32), starts_ref)
    pieces = []
    for k in range(chunks):
        rows = slice(k * CHUNK, (k + 1) * CHUNK)
        raw = control_ref[rows, 2 * STATE :].astype(f32) + par_ref[0:1, :]
        step = jnp.maximum(raw, 0.0) + jnp.log1p(jnp.exp(-jnp.abs(raw)))
        log_step = jnp.log(step)
        log_rate = -par_ref[1:2, :] * step
        cum = jnp.dot(tri, log_rate, precision=highest, preferred_element_type=f32)
        before = cum - log_rate
        whole = cum[CHUNK - 1 : CHUNK, :]
        cola_ref[rows, :] = cum
        colb_ref[rows, :] = before
        rowf_ref[k] = jnp.transpose(cum - log_step)[:heads]
        rowb_ref[k] = jnp.transpose(before + log_step)[:heads]
        seg = segment_of(base + k * CHUNK + iota((CHUNK, 1), 0), starts_ref)
        first, last = seg_at(k * CHUNK), seg_at((k + 1) * CHUNK - 1)
        prior, after = seg_at(k * CHUNK - 1), seg_at((k + 1) * CHUNK)
        w_f = jnp.where(seg == last, step * jnp.exp(whole - cum), 0.0)
        w_b = jnp.where(seg == first, step * jnp.exp(before), 0.0)
        b_in = control_ref[rows, :STATE]
        wide = values_ref[rows, :].astype(f32)
        add_f = mm_tn(b_in, (wide * expand(w_f, spread)).astype(bf16))
        add_b = mm_tn(b_in, (wide * expand(w_b, spread)).astype(bf16))
        keep = jnp.exp(whole)
        keep_f = jnp.where(prior == last, keep, 0.0)
        keep_b = jnp.where(first == after, keep, 0.0)
        pieces.append((seg, cum, before, whole, add_f, add_b, keep_f, keep_b))
    lift = lambda w: expand(jnp.broadcast_to(w, (8, LANES)), spread)[0:1]
    for d, order in enumerate((range(chunks), range(chunks - 1, -1, -1))):
        state = jnp.zeros((STATE, cols), f32)
        keep_all = jnp.ones((1, LANES), f32)
        shift = jnp.zeros((1, LANES), f32)
        edge = seg_at(-1) if d == 0 else seg_at(tokens)
        for k in order:
            seg, cum, before, whole, add_f, add_b, keep_f, keep_b = pieces[k]
            pre_ref[d, k] = state.astype(bf16)
            add, keep = (add_f, keep_f) if d == 0 else (add_b, keep_b)
            inner = cum if d == 0 else whole - before
            reach_ref[d, k * CHUNK : (k + 1) * CHUNK, :] = jnp.where(
                seg == edge, jnp.exp(inner + shift), 0.0
            )
            state = lift(keep) * state + add
            keep_all = keep_all * keep
            shift = shift + whole
        total_ref[d, :STATE] = state.astype(bf16)
        total_ref[d, STATE:] = jnp.broadcast_to(lift(keep_all), (KEEP_ROWS, cols)).astype(bf16)


def chunk_states(starts, base, control, values, par):
    tokens, cols = values.shape
    chunks, heads = tokens // CHUNK, cols // HEAD_DIM
    shapes = [
        ((2, STATE + KEEP_ROWS, cols), bf16),
        ((2, chunks, STATE, cols), bf16),
        ((tokens, LANES), f32),
        ((tokens, LANES), f32),
        ((chunks, heads, CHUNK), f32),
        ((chunks, heads, CHUNK), f32),
        ((2, tokens, LANES), f32),
    ]
    return pl.pallas_call(
        states_kernel,
        grid=(1,),
        in_specs=[SMEM, SMEM, full(control.shape), full(values.shape), full(par.shape)],
        out_specs=[full(s) for s, _ in shapes],
        out_shape=[jax.ShapeDtypeStruct(s, t) for s, t in shapes],
        name="chunk_states",
    )(starts, base, control, values, par)


def within_kernel(
    starts_ref, base_ref, control_ref, values_ref, skip_ref,
    pre_ref, cola_ref, colb_ref, rowf_ref, rowb_ref, out_ref,
):
    cols = values_ref.shape[1]
    k = pl.program_id(0)
    start = base_ref[0] + k * CHUNK
    spread = expander(cols)
    row, col = iota((CHUNK, CHUNK), 0), iota((CHUNK, CHUNK), 1)
    low_lanes = iota((CHUNK, LANES), 1) < HEAD_DIM
    b_in, c_out = control_ref[:, :STATE], control_ref[:, STATE : 2 * STATE]
    seg_col = segment_of(start + iota((CHUNK, 1), 0), starts_ref)
    seg_row = segment_of(start + iota((1, CHUNK), 1), starts_ref)
    prior = segment_of(jnp.full((1, 1), start - 1, jnp.int32), starts_ref)
    after = segment_of(jnp.full((1, 1), start + CHUNK, jnp.int32), starts_ref)
    same = seg_col == seg_row
    lower = row >= col
    scores = mm_nt(c_out, b_in)
    scores_f = jnp.where(lower & same, scores, 0.0)
    scores_b = jnp.where((row <= col) & same, scores, 0.0)
    cum, before = cola_ref[...], colb_ref[...]
    whole = cum[CHUNK - 1 : CHUNK, :]
    far_f = expand(jnp.where(seg_col == prior, jnp.exp(cum), 0.0), spread)
    far_b = expand(jnp.where(seg_col == after, jnp.exp(whole - before), 0.0), spread)
    carry_f = mm(c_out, pre_ref[0, 0]) * far_f
    carry_b = mm(c_out, pre_ref[1, 0]) * far_b
    per_tile = LANES // HEAD_DIM
    for pair in range(cols // LANES):
        lanes = slice(pair * LANES, (pair + 1) * LANES)
        value = values_ref[:, lanes]
        left_f, left_b = [], []
        for h in range(pair * per_tile, (pair + 1) * per_tile):
            gap = jnp.where(
                lower,
                cum[:, h : h + 1] - rowf_ref[0, h : h + 1, :],
                rowb_ref[0, h : h + 1, :] - before[:, h : h + 1],
            )
            weight = jnp.exp(gap)
            left_f.append((weight * scores_f).astype(bf16))
            left_b.append((weight * scores_b).astype(bf16))
        left = jnp.concatenate(
            [jnp.concatenate(left_f, axis=1), jnp.concatenate(left_b, axis=1)], axis=0
        )
        zero = jnp.zeros_like(value)
        right = jnp.concatenate(
            [jnp.where(low_lanes, value, zero), jnp.where(low_lanes, zero, value)], axis=0
        )
        near = mm(left, right)
        direct = value.astype(f32) * skip_ref[:, lanes]
        out_ref[0, :, lanes] = near[:CHUNK] + carry_f[:, lanes] + direct
        out_ref[1, :, lanes] = near[CHUNK:] + carry_b[:, lanes] + direct


def within(starts, base, control, values, skip_row, pre, cola, colb, rowf, rowb):
    tokens, cols = values.shape
    chunks, heads = tokens // CHUNK, cols // HEAD_DIM
    rows = lambda width: pl.BlockSpec((CHUNK, width), lambda k: (k, 0))
    return pl.pallas_call(
        within_kernel,
        grid=(chunks,),
        in_specs=[
            SMEM, SMEM,
            rows(control.shape[1]), rows(cols), full(skip_row.shape),
            pl.BlockSpec((2, 1, STATE, cols), lambda k: (0, k, 0, 0)),
            rows(LANES), rows(LANES),
            pl.BlockSpec((1, heads, CHUNK), lambda k: (k, 0, 0)),
            pl.BlockSpec((1, heads, CHUNK), lambda k: (k, 0, 0)),
        ],
        out_specs=pl.BlockSpec((2, CHUNK, cols), lambda k: (0, k, 0)),
        out_shape=jax.ShapeDtypeStruct((2, tokens, cols), f32),
        name="within_chunk",
    )(starts, base, control, values, skip_row, pre, cola, colb, rowf, rowb)


def gate_kernel(control_ref, near_ref, into_ref, reach_ref, gates_ref, out_ref, squares_ref):
    cols = gates_ref.shape[1]
    spread = expander(cols)
    c_out = control_ref[:, STATE : 2 * STATE]
    gate = gates_ref[...].astype(f32)
    active = gate * jax.nn.sigmoid(gate)
    lane = iota((CHUNK, LANES), 1)
    squares = jnp.zeros((CHUNK, LANES), f32)
    for d in range(2):
        carry = mm(c_out, into_ref[d]) * expand(reach_ref[d], spread)
        y = (near_ref[d] + carry).astype(bf16).astype(f32)
        v = y * active
        squares = jnp.where(lane == d, jnp.sum(v * v, axis=1, keepdims=True), squares)
        out_ref[d] = v.astype(bf16)
    squares_ref[...] = jnp.transpose(squares)[:8]


def carry_gate(control, near, into, reach, gates):
    tokens, cols = gates.shape
    rows = lambda width: pl.BlockSpec((CHUNK, width), lambda k: (k, 0))
    both = lambda width: pl.BlockSpec((2, CHUNK, width), lambda k: (0, k, 0))
    return pl.pallas_call(
        gate_kernel,
        grid=(tokens // CHUNK,),
        in_specs=[rows(control.shape[1]), both(cols), full(into.shape), both(LANES), rows(cols)],
        out_specs=[both(cols), pl.BlockSpec((8, CHUNK), lambda k: (0, k))],
        out_shape=[
            jax.ShapeDtypeStruct((2, tokens, cols), bf16),
            jax.ShapeDtypeStruct((8, tokens), f32),
        ],
        name="carry_gate",
    )(control, near, into, reach, gates)


def output_kernel(inner, sums, mirror_ref, gated_ref, *refs):
    squares_refs = refs[:sums]
    gain_ref, wa_ref, wb_ref, out_ref = refs[sums:]
    squares = squares_refs[0][...]
    for other in squares_refs[1:]:
        squares = squares + other[...]
    scale = lax.rsqrt(squares / inner + norm_eps)
    scale = jnp.transpose(jnp.concatenate([scale, jnp.zeros((CHUNK - 8, CHUNK), f32)], axis=0))
    gain = gain_ref[...]
    combined = (
        gated_ref[0].astype(f32) * scale[:, 0:1] * gain
        + gated_ref[1].astype(f32) * scale[:, 1:2] * gain
    ).astype(bf16)
    cols = wa_ref.shape[0]
    product = mm(combined[:, :cols], wa_ref[...]) + mm(combined[:, cols:], wb_ref[...])
    product = product.astype(bf16)
    slots, _, width = out_ref.shape
    blocks, per_slot = slots * width // REV, width // REV

    @pl.when(mirror_ref[0] == 0)
    def _():
        for j in range(slots):
            out_ref[j] = product[:, j * width : (j + 1) * width]

    @pl.when(mirror_ref[0] == 1)
    def _():
        swap = exchange_matrix(jnp.int32(1))
        for q in range(blocks):
            j, at = divmod(blocks - 1 - q, per_slot)
            out_ref[j, :, at * REV : (at + 1) * REV] = mm(
                product[:, q * REV : (q + 1) * REV], swap
            ).astype(bf16)


def output_project(inner, mirror, gated, squares, gain_row, weights, slots, piece, pieces):
    _, tokens, cols = gated.shape
    width = weights[0].shape[1] // slots
    steps = tokens // CHUNK // pieces
    at = lambda k: k + piece * steps
    return pl.pallas_call(
        functools.partial(output_kernel, inner, len(squares)),
        grid=(steps,),
        in_specs=[SMEM, pl.BlockSpec((2, CHUNK, cols), lambda k: (0, at(k), 0))]
        + [pl.BlockSpec((8, CHUNK), lambda k: (0, at(k))) for _ in squares]
        + [full(gain_row.shape)]
        + [full(w.shape) for w in weights],
        out_specs=pl.BlockSpec((slots, CHUNK, width), lambda k: (0, k, 0)),
        out_shape=jax.ShapeDtypeStruct((slots, tokens // pieces, width), bf16),
        name="output_project",
    )(mirror, gated, *squares, gain_row, *weights)


def incoming_states(total):
    count = lax.axis_size("seq")
    late = lax.axis_index("seq") % 2 == 1
    state = lambda m: m[:STATE].astype(f32)
    keep = lambda m: m[STATE : STATE + 1].astype(f32)
    swap = [(i, i ^ 1) for i in range(count)]
    mine = jnp.where(late, total[0], total[1])
    near = lax.ppermute(jnp.where(late, total[1], total[0]), "seq", swap)
    pair = jnp.concatenate(
        [
            keep(mine) * state(near) + state(mine),
            jnp.broadcast_to(keep(mine) * keep(near), (KEEP_ROWS, total.shape[2])),
        ],
        axis=0,
    ).astype(bf16)
    into, decay = 0.0, 1.0
    for k in range(1, count // 2):
        hop = [(i, i + 2 * k) for i in range(1, count, 2) if i + 2 * k < count]
        hop += [(i, i - 2 * k) for i in range(0, count, 2) if i - 2 * k >= 0]
        got = lax.ppermute(pair, "seq", hop)
        into = into + decay * state(got)
        decay = decay * keep(got)
    across = lax.ppermute(into.astype(bf16), "seq", swap)
    through = (keep(near) * into + state(near)).astype(bf16)
    return jnp.stack([jnp.where(late, through, across), jnp.where(late, across, through)])


def chan_parts(part):
    count = lax.axis_size("chan")
    return [part] + [
        lax.ppermute(part, "chan", [(i, (i + 2 * k) % count) for i in range(count)])
        for k in range(1, count // 2)
    ]


def settled(x):
    def kernel(x_ref, out_ref):
        out_ref[...] = x_ref[...]

    return pl.pallas_call(
        kernel, out_shape=jax.ShapeDtypeStruct(x.shape, x.dtype), name="settled"
    )(x)


def shard_of(rank, turn, count):
    slots = count // 2
    return rank % 2 * slots + (rank // 2 + turn) % slots


def turns(count, back):
    for turn in range(count // 2):
        pairs = [(shard_of(r, turn, count), r) for r in range(count)]
        yield turn, [(b, a) if back else (a, b) for a, b in pairs if a != b]


def gather_strand(hidden, count):
    slots = count // 2
    xs = [hidden] + [lax.ppermute(hidden, "chan", pairs) for _, pairs in turns(count, False)]
    routes = []
    for rank in range(count):
        by_slot = [None] * slots
        for turn in range(slots):
            shard = shard_of(rank, turn, count)
            by_slot[shard % slots] = [0 if shard == rank else 1 + turn]
        routes.append(by_slot)
    return routes, xs


def reduce_strand(partial, count, rank):
    slots = count // 2
    total = 0.0
    for turn, pairs in turns(count, True):
        mine = lax.dynamic_index_in_dim(partial, (rank // 2 + turn) % slots, 0, False)
        got = lax.ppermute(mine, "chan", pairs)
        kept = shard_of(rank, turn, count) == rank
        total = total + jnp.where(kept, mine, got).astype(f32)
    return total.astype(bf16)


def partner_weights(w, count):
    rows = w.shape[0] // lax.axis_size("seq")
    part = lax.dynamic_slice_in_dim(w, lax.axis_index("seq") * rows, rows, 0)
    part = lax.ppermute(part, "chan", [(i, i ^ 1) for i in range(count)])
    return lax.all_gather(part, "seq", axis=0, tiled=True)


def local(
    hidden, norm_gain, w_values, w_gates, w_control, dt_bias, decay_total, skip_gain, gate_gain,
    w_out, doc_starts,
):
    seq_count, chan_count = lax.axis_size("seq"), lax.axis_size("chan")
    seq_rank, chan_rank = lax.axis_index("seq"), lax.axis_index("chan")
    tokens = hidden.shape[0]
    cols = w_values.shape[1]
    heads = cols // HEAD_DIM
    slots = chan_count // 2

    def mine(a, axis):
        return jnp.concatenate(
            [
                lax.dynamic_slice_in_dim(a, rank * heads, heads, axis)
                for rank in (chan_rank, chan_rank ^ 1)
            ],
            axis,
        )

    lanes = lambda a: jnp.pad(a, ((0, 0), (0, LANES - 2 * heads)))
    routes, xs = gather_strand(hidden, chan_count)
    values_w = (w_values, partner_weights(w_values, chan_count))
    gates_w = (w_gates, partner_weights(w_gates, chan_count))
    out_w = (w_out, partner_weights(w_out, chan_count))
    swap = [(i, i ^ 1) for i in range(chan_count)]
    gate_row = jnp.concatenate([gate_gain, lax.ppermute(gate_gain, "chan", swap)])[None]
    w_small = jnp.concatenate(
        [w_control[:, : 2 * STATE], lanes(mine(w_control[:, 2 * STATE :], 1))], axis=1
    )
    par = lanes(jnp.stack([mine(dt_bias, 0), mine(decay_total, 0) / (tokens * seq_count)]))
    par = jnp.pad(par, ((0, 6), (0, 0)))
    par = settled(par)
    skip_row = jnp.repeat(mine(skip_gain, 0), HEAD_DIM)[None]
    scalar = lambda v: jnp.reshape(v, (1,)).astype(jnp.int32)
    base, mirror = scalar(seq_rank * tokens), scalar(chan_rank % 2)
    normed, values, control = norm_project(
        routes, xs, scalar(chan_rank), mirror, norm_gain[None], values_w, w_small
    )
    total, pre, cola, colb, rowf, rowb, reach = chunk_states(doc_starts, base, control, values, par)
    into = incoming_states(total)
    gates = project(normed, gates_w)
    near = within(doc_starts, base, control, values, skip_row, pre, cola, colb, rowf, rowb)
    gated, squares = carry_gate(control, near, into, reach, gates)
    sums = chan_parts(squares)
    result = []
    for p in range(PIECES):
        out = output_project(
            cols * chan_count, mirror, gated, sums, gate_row, out_w, slots, p, PIECES
        )
        result.append(reduce_strand(out, chan_count, chan_rank))
    return jnp.concatenate(result, axis=0)


def solution(mesh):
    in_specs = (
        P("seq", "chan"), P(), P(None, "chan"), P(None, "chan"), P(), P(), P(), P(), P("chan"),
        P("chan", None), P(),
    )
    return jax.shard_map(
        local, mesh=mesh, in_specs=in_specs, out_specs=P("seq", "chan"), check_vma=False
    )
```

```python
import functools

import jax
import jax.numpy as jnp
from jax import lax
from jax.experimental import pallas as pl
from jax.experimental.pallas import tpu as pltpu
from jax.sharding import PartitionSpec as P


HEAD_DIM = 64
STATE = 128
CHUNK = 128
LANES = 128
REV = 256
TILE = 512
KEEP_ROWS = 16
PIECES = 2


norm_eps = 1e-05
highest = lax.Precision.HIGHEST
f32 = jnp.float32
bf16 = jnp.bfloat16


def mm(a, b):
    return jnp.dot(a, b, preferred_element_type=f32)


def mm_nt(a, b):
    return lax.dot_general(a, b, (((1,), (1,)), ((), ())), preferred_element_type=f32)


def mm_tn(a, b):
    return lax.dot_general(a, b, (((0,), (0,)), ((), ())), preferred_element_type=f32)


def iota(shape, dim):
    return lax.broadcasted_iota(jnp.int32, shape, dim)


def exchange_matrix(mirror):
    row, col = iota((REV, REV), 0), iota((REV, REV), 1)
    return (row == jnp.where(mirror == 1, REV - 1 - col, col)).astype(f32).astype(bf16)


def segment_of(position, starts_ref):
    total = jnp.zeros_like(position)
    for k in range(starts_ref.shape[0]):
        total = total + (position >= starts_ref[k]).astype(jnp.int32)
    return total


def expander(width, first=0):
    row, col = iota((2 * LANES, width), 0), first + iota((2 * LANES, width), 1)
    return ((row % LANES) == (col // HEAD_DIM)).astype(f32).astype(bf16)


def halves(w):
    high = w.astype(bf16)
    low = (w - high.astype(f32)).astype(bf16)
    return jnp.concatenate([high, low], axis=1)


def expand(w, spread):
    return mm(halves(w), spread)


def full(shape):
    return pl.BlockSpec(shape, lambda *_: (0,) * len(shape))


SMEM = pl.BlockSpec(memory_space=pltpu.SMEM)


def norm_project_kernel(routes, rank_ref, mirror_ref, *refs):
    slots, pieces = len(routes[0]), len(routes[0][0])
    xs = refs[: 1 + max(at for by_slot in routes for row in by_slot for at in row)]
    gain_ref, wa_ref, wb_ref, wc_ref, normed_ref, values_ref, control_ref, scr, held, sems = refs[
        len(xs) :
    ]
    half = normed_ref.shape[1]
    blocks = half // REV
    _, tokens, width = held.shape
    rows = tokens // pieces

    @pl.when(pl.program_id(0) == 0)
    def _():
        rank, mirror = rank_ref[0], mirror_ref[0]
        target = lambda j, p: held.at[j, pl.ds(p * rows, rows), :]
        for r, by_slot in enumerate(routes):

            @pl.when(rank == r)
            def _():
                for j in range(slots):
                    for p in range(pieces):
                        pltpu.make_async_copy(
                            xs[by_slot[j][p]], target(j, p), sems.at[j, p]
                        ).start()

        swap = exchange_matrix(mirror)
        squares = jnp.zeros((tokens, 1), f32)
        at = 0
        for j in range(slots):
            for p in range(pieces):
                pltpu.make_async_copy(xs[0], target(j, p), sems.at[j, p]).wait()
            for q in range(width // REV):
                xb = held[j, :, q * REV : (q + 1) * REV]
                wide = xb.astype(f32)
                squares = squares + jnp.sum(wide * wide, axis=1, keepdims=True)
                scr[jnp.where(mirror == 1, blocks - 1 - at, at)] = mm(xb, swap).astype(bf16)
                at += 1
        scale = lax.rsqrt(squares / half + norm_eps)
        for q in range(blocks):
            cols = slice(q * REV, (q + 1) * REV)
            normed_ref[:, cols] = (scr[q].astype(f32) * scale * gain_ref[:, cols]).astype(bf16)
        control_ref[...] = mm(normed_ref[...], wc_ref[...]).astype(bf16)

    two_weights(normed_ref, wa_ref, wb_ref, values_ref)


def two_weights(x_ref, wa_ref, wb_ref, out_ref):
    first = pl.program_id(0) < pl.num_programs(0) // 2

    @pl.when(first)
    def _():
        out_ref[...] = mm(x_ref[...], wa_ref[...]).astype(bf16)

    @pl.when(jnp.logical_not(first))
    def _():
        out_ref[...] = mm(x_ref[...], wb_ref[...]).astype(bf16)


def weight_specs(half, tile, steps):
    return [
        pl.BlockSpec((half, tile), lambda j: (0, jnp.minimum(j, steps - 1))),
        pl.BlockSpec((half, tile), lambda j: (0, jnp.maximum(j - steps, 0))),
    ]


def gates_kernel(x_ref, wa_ref, wb_ref, out_ref):
    first = pl.program_id(0) < pl.num_programs(0) // 2

    def activate(w_ref):
        gate = mm(x_ref[...], w_ref[...]).astype(bf16).astype(f32)
        out_ref[...] = (gate * jax.nn.sigmoid(gate)).astype(bf16)

    pl.when(first)(lambda: activate(wa_ref))
    pl.when(jnp.logical_not(first))(lambda: activate(wb_ref))


def activated_gates(x, weights):
    tokens, half = x.shape
    cols = weights[0].shape[1]
    tile = min(TILE, cols)
    steps = cols // tile
    return pl.pallas_call(
        gates_kernel,
        grid=(2 * steps,),
        in_specs=[full(x.shape)] + weight_specs(half, tile, steps),
        out_specs=pl.BlockSpec((tokens, tile), lambda j: (0, j)),
        out_shape=jax.ShapeDtypeStruct((tokens, 2 * cols), bf16),
        name="activated_gates",
    )(x, *weights)


def norm_project(routes, xs, rank, mirror, gain, weights, w_control):
    slots, pieces = len(routes[0]), len(routes[0][0])
    tokens = xs[0].shape[0] * pieces
    half, cols = weights[0].shape
    tile = min(TILE, cols)
    steps = cols // tile
    return pl.pallas_call(
        functools.partial(norm_project_kernel, routes),
        grid=(2 * steps,),
        in_specs=[SMEM, SMEM]
        + [pl.BlockSpec(memory_space=pl.ANY) for x in xs]
        + [full(gain.shape)]
        + weight_specs(half, tile, steps)
        + [full(w_control.shape)],
        out_specs=[
            full((tokens, half)),
            pl.BlockSpec((tokens, tile), lambda j: (0, j)),
            full((tokens, w_control.shape[1])),
        ],
        out_shape=[
            jax.ShapeDtypeStruct((tokens, half), bf16),
            jax.ShapeDtypeStruct((tokens, 2 * cols), bf16),
            jax.ShapeDtypeStruct((tokens, w_control.shape[1]), bf16),
        ],
        scratch_shapes=[
            pltpu.VMEM((half // REV, tokens, REV), bf16),
            pltpu.VMEM((slots, tokens, half // slots), bf16),
            pltpu.SemaphoreType.DMA((slots, pieces)),
        ],
        name="norm_project",
    )(rank, mirror, *xs, gain, *weights, w_control)


def states_kernel(
    starts_ref, base_ref, control_ref, values_ref, par_ref,
    total_ref, pre_ref, cola_ref, colb_ref, rowf_ref, rowb_ref, reach_ref,
    weights_ref, keeps_ref,
):
    tokens, cols = values_ref.shape
    chunks = tokens // CHUNK
    j = pl.program_id(0)

    @pl.when(j == 0)
    def _():
        step_terms(
            starts_ref, base_ref, control_ref, par_ref,
            cola_ref, colb_ref, rowf_ref, rowb_ref, reach_ref, weights_ref, keeps_ref,
        )

    tile = 256
    for at in range(0, cols, tile):
        lanes = slice(at, at + tile)
        spread = expander(tile, j * cols + at)
        lifted = mm(keeps_ref[...], spread)
        wide = values_ref[:, lanes].astype(f32)
        for d, order in enumerate((range(chunks), range(chunks - 1, -1, -1))):
            scaled = (wide * mm(weights_ref[d], spread)).astype(bf16)
            state = jnp.zeros((STATE, tile), f32)
            for i, k in enumerate(order):
                rows = slice(k * CHUNK, (k + 1) * CHUNK)
                pre_ref[d, k, :, lanes] = state.astype(bf16)
                line = d * (chunks + 1) + i
                state = lifted[line : line + 1] * state + mm_tn(
                    control_ref[rows, :STATE], scaled[rows]
                )
            total_ref[d, :STATE, lanes] = state.astype(bf16)
            line = d * (chunks + 1) + chunks
            total_ref[d, STATE:, lanes] = jnp.broadcast_to(
                lifted[line : line + 1], (KEEP_ROWS, tile)
            ).astype(bf16)


def step_terms(
    starts_ref, base_ref, control_ref, par_ref,
    cola_ref, colb_ref, rowf_ref, rowb_ref, reach_ref, weights_ref, keeps_ref,
):
    tokens = control_ref.shape[0]
    chunks, heads = rowf_ref.shape[:2]
    base = base_ref[0]
    row, col = iota((CHUNK, CHUNK), 0), iota((CHUNK, CHUNK), 1)
    tri = (row >= col).astype(f32)
    seg_at = lambda offset: segment_of(base + jnp.full((1, 1), offset, jnp.int32), starts_ref)
    small, weights = [], [[], []]
    for k in range(chunks):
        rows = slice(k * CHUNK, (k + 1) * CHUNK)
        raw = control_ref[rows, 2 * STATE :].astype(f32) + par_ref[0:1, :]
        step = jnp.maximum(raw, 0.0) + jnp.log1p(jnp.exp(-jnp.abs(raw)))
        log_step = jnp.log(step)
        log_rate = -par_ref[1:2, :] * step
        cum = jnp.dot(tri, log_rate, precision=highest, preferred_element_type=f32)
        before = cum - log_rate
        whole = cum[CHUNK - 1 : CHUNK, :]
        cola_ref[rows, :] = cum
        colb_ref[rows, :] = before
        rowf_ref[k] = jnp.transpose(cum - log_step)[:heads]
        rowb_ref[k] = jnp.transpose(before + log_step)[:heads]
        seg = segment_of(base + k * CHUNK + iota((CHUNK, 1), 0), starts_ref)
        first, last = seg_at(k * CHUNK), seg_at((k + 1) * CHUNK - 1)
        prior, after = seg_at(k * CHUNK - 1), seg_at((k + 1) * CHUNK)
        weights[0].append(jnp.where(seg == last, step * jnp.exp(whole - cum), 0.0))
        weights[1].append(jnp.where(seg == first, step * jnp.exp(before), 0.0))
        keep = jnp.exp(whole)
        keeps = (jnp.where(prior == last, keep, 0.0), jnp.where(first == after, keep, 0.0))
        small.append((seg, cum, whole - before, whole, keeps))
    keep_rows = []
    orders = (range(chunks), range(chunks - 1, -1, -1))
    for d, order in enumerate(orders):
        keep_all = jnp.ones((1, LANES), f32)
        shift = jnp.zeros((1, LANES), f32)
        edge = seg_at(-1) if d == 0 else seg_at(tokens)
        for k in order:
            seg, whole = small[k][0], small[k][3]
            reach_ref[d, k * CHUNK : (k + 1) * CHUNK, :] = jnp.where(
                seg == edge, jnp.exp(small[k][1 + d] + shift), 0.0
            )
            keep_rows.append(small[k][4][d])
            keep_all = keep_all * small[k][4][d]
            shift = shift + whole
        keep_rows.append(keep_all)
    padding = keeps_ref.shape[0] - len(keep_rows)
    keeps_ref[...] = halves(jnp.concatenate(keep_rows + [jnp.zeros((padding, LANES), f32)], axis=0))
    for d in range(2):
        weights_ref[d] = halves(jnp.concatenate(weights[d], axis=0))


def chunk_states(starts, base, control, values, par):
    tokens, cols = values.shape
    chunks, heads = tokens // CHUNK, cols // HEAD_DIM
    shapes = [
        ((2, STATE + KEEP_ROWS, cols), bf16),
        ((2, chunks, STATE, cols), bf16),
        ((tokens, LANES), f32),
        ((tokens, LANES), f32),
        ((chunks, heads, CHUNK), f32),
        ((chunks, heads, CHUNK), f32),
        ((2, tokens, LANES), f32),
    ]
    steps = 2 if cols % 512 == 0 else 1
    width = cols // steps
    specs = [
        pl.BlockSpec((2, STATE + KEEP_ROWS, width), lambda j: (0, 0, j)),
        pl.BlockSpec((2, chunks, STATE, width), lambda j: (0, 0, 0, j)),
    ] + [full(shape) for shape, _ in shapes[2:]]
    return pl.pallas_call(
        states_kernel,
        grid=(steps,),
        in_specs=[
            SMEM, SMEM, full(control.shape), pl.BlockSpec((tokens, width), lambda j: (0, j)),
            full(par.shape),
        ],
        out_specs=specs,
        out_shape=[jax.ShapeDtypeStruct(s, t) for s, t in shapes],
        scratch_shapes=[
            pltpu.VMEM((2, tokens, 2 * LANES), bf16),
            pltpu.VMEM((-(-2 * (chunks + 1) // 16) * 16, 2 * LANES), bf16),
        ],
        name="chunk_states",
    )(starts, base, control, values, par)


def within_kernel(
    starts_ref, base_ref, control_ref, values_ref, skip_ref,
    pre_ref, cola_ref, colb_ref, rowf_ref, rowb_ref, out_ref,
):
    per_step = values_ref.shape[0] // CHUNK
    spread = expander(values_ref.shape[1])
    for i in range(per_step):
        rows = pl.ds(i * CHUNK, CHUNK)
        start = base_ref[0] + (pl.program_id(0) * per_step + i) * CHUNK
        within_chunk(
            starts_ref, start, control_ref.at[rows], values_ref.at[rows], skip_ref,
            pre_ref.at[:, pl.ds(i, 1)], cola_ref.at[rows], colb_ref.at[rows],
            rowf_ref.at[pl.ds(i, 1)], rowb_ref.at[pl.ds(i, 1)], out_ref.at[:, rows], spread,
        )


def within_chunk(
    starts_ref, start, control_ref, values_ref, skip_ref,
    pre_ref, cola_ref, colb_ref, rowf_ref, rowb_ref, out_ref, spread,
):
    cols = values_ref.shape[1]
    row, col = iota((CHUNK, CHUNK), 0), iota((CHUNK, CHUNK), 1)
    low_lanes = iota((CHUNK, LANES), 1) < HEAD_DIM
    b_in, c_out = control_ref[:, :STATE], control_ref[:, STATE : 2 * STATE]
    seg_col = segment_of(start + iota((CHUNK, 1), 0), starts_ref)
    seg_row = segment_of(start + iota((1, CHUNK), 1), starts_ref)
    prior = segment_of(jnp.full((1, 1), start - 1, jnp.int32), starts_ref)
    after = segment_of(jnp.full((1, 1), start + CHUNK, jnp.int32), starts_ref)
    same = seg_col == seg_row
    lower = row >= col
    scores = mm_nt(c_out, b_in)
    scores_f = jnp.where(lower & same, scores, 0.0)
    scores_b = jnp.where((row <= col) & same, scores, 0.0)
    cum, before = cola_ref[...], colb_ref[...]
    whole = cum[CHUNK - 1 : CHUNK, :]
    far_f = expand(jnp.where(seg_col == prior, jnp.exp(cum), 0.0), spread)
    far_b = expand(jnp.where(seg_col == after, jnp.exp(whole - before), 0.0), spread)
    carry_f = mm(c_out, pre_ref[0, 0]) * far_f
    carry_b = mm(c_out, pre_ref[1, 0]) * far_b
    per_tile = LANES // HEAD_DIM
    for pair in range(cols // LANES):
        lanes = slice(pair * LANES, (pair + 1) * LANES)
        value = values_ref[:, lanes]
        left_f, left_b = [], []
        for h in range(pair * per_tile, (pair + 1) * per_tile):
            gap = jnp.where(
                lower,
                cum[:, h : h + 1] - rowf_ref[0, h : h + 1, :],
                rowb_ref[0, h : h + 1, :] - before[:, h : h + 1],
            )
            weight = jnp.exp(gap)
            left_f.append((weight * scores_f).astype(bf16))
            left_b.append((weight * scores_b).astype(bf16))
        left = jnp.concatenate(
            [jnp.concatenate(left_f, axis=1), jnp.concatenate(left_b, axis=1)], axis=0
        )
        zero = jnp.zeros_like(value)
        right = jnp.concatenate(
            [jnp.where(low_lanes, value, zero), jnp.where(low_lanes, zero, value)], axis=0
        )
        near = mm(left, right)
        direct = value.astype(f32) * skip_ref[:, lanes]
        out_ref[0, :, lanes] = (near[:CHUNK] + carry_f[:, lanes] + direct).astype(bf16)
        out_ref[1, :, lanes] = (near[CHUNK:] + carry_b[:, lanes] + direct).astype(bf16)


def within(starts, base, control, values, skip_row, pre, cola, colb, rowf, rowb):
    tokens, cols = values.shape
    chunks, heads = tokens // CHUNK, cols // HEAD_DIM
    n = 1
    rows = lambda width: pl.BlockSpec((n * CHUNK, width), lambda k: (k, 0))
    return pl.pallas_call(
        within_kernel,
        grid=(chunks // n,),
        in_specs=[
            SMEM, SMEM,
            rows(control.shape[1]), rows(cols), full(skip_row.shape),
            pl.BlockSpec((2, n, STATE, cols), lambda k: (0, k, 0, 0)),
            rows(LANES), rows(LANES),
            pl.BlockSpec((n, heads, CHUNK), lambda k: (k, 0, 0)),
            pl.BlockSpec((n, heads, CHUNK), lambda k: (k, 0, 0)),
        ],
        out_specs=pl.BlockSpec((2, n * CHUNK, cols), lambda k: (0, k, 0)),
        out_shape=jax.ShapeDtypeStruct((2, tokens, cols), bf16),
        name="within_chunk",
    )(starts, base, control, values, skip_row, pre, cola, colb, rowf, rowb)


def gate_kernel(control_ref, near_ref, into_ref, reach_ref, active_ref, out_ref, squares_ref, acc):
    tile = active_ref.shape[1]
    rows = active_ref.shape[0]
    j = pl.program_id(0)
    spread = expander(tile, j * tile)
    c_out = control_ref[...]
    active = active_ref[...].astype(f32)
    lane = iota((rows, LANES), 1)
    total = jnp.where(j == 0, 0.0, acc[...])
    for d in range(2):
        carry = mm(c_out, into_ref[d]) * expand(reach_ref[d], spread)
        v = (near_ref[d].astype(f32) + carry) * active
        total = total + jnp.where(lane == d, jnp.sum(v * v, axis=1, keepdims=True), 0.0)
        out_ref[d] = v.astype(bf16)
    acc[...] = total

    @pl.when(j == pl.num_programs(0) - 1)
    def _():
        squares_ref[...] = jnp.transpose(acc[...])[:8]


def carry_gate(control, near, into, reach, active, piece, pieces):
    tokens, cols = active.shape
    rows = tokens // pieces
    tile = min(1024, cols)
    return pl.pallas_call(
        gate_kernel,
        grid=(cols // tile,),
        in_specs=[
            pl.BlockSpec((rows, STATE), lambda j: (piece, 1)),
            pl.BlockSpec((2, rows, tile), lambda j: (0, piece, j)),
            pl.BlockSpec((2, STATE, tile), lambda j: (0, 0, j)),
            pl.BlockSpec((2, rows, LANES), lambda j: (0, piece, 0)),
            pl.BlockSpec((rows, tile), lambda j: (piece, j)),
        ],
        out_specs=[
            pl.BlockSpec((2, rows, tile), lambda j: (0, 0, j)),
            pl.BlockSpec((8, rows), lambda j: (0, 0)),
        ],
        out_shape=[
            jax.ShapeDtypeStruct((2, rows, cols), bf16),
            jax.ShapeDtypeStruct((8, rows), f32),
        ],
        scratch_shapes=[pltpu.VMEM((rows, LANES), f32)],
        name="carry_gate",
    )(control, near, into, reach, active)


def split_mm(parity, x_ref, first, near_ref, far_ref):
    rows = near_ref.shape[0]
    cols = lambda half: pl.ds(pl.multiple_of(first + half * rows, rows), rows)
    return mm(x_ref[:, cols(parity)], near_ref[...]) + mm(x_ref[:, cols(1 - parity)], far_ref[...])


def output_kernel(inner, sums, place_ref, gated_ref, *refs):
    squares_refs = refs[:sums]
    gain_ref, wa_ref, near_ref, far_ref, out_ref, combined = refs[sums:]
    rows, tile = out_ref.shape

    @pl.when(pl.program_id(0) == 0)
    def _():
        squares = squares_refs[0][...]
        for other in squares_refs[1:]:
            squares = squares + other[...]
        scale = lax.rsqrt(squares / inner + norm_eps)
        scale = jnp.concatenate([scale, jnp.zeros((LANES - 8, rows), f32)], axis=0)
        scale = jnp.transpose(scale)
        combined[...] = (
            (
                gated_ref[0].astype(f32) * scale[:, 0:1]
                + gated_ref[1].astype(f32) * scale[:, 1:2]
            )
            * gain_ref[...]
        ).astype(bf16)

    cols = wa_ref.shape[0]
    product = mm(combined[:, :cols], wa_ref[...])
    product = (product + split_mm(place_ref[2], combined, cols, near_ref, far_ref)).astype(bf16)

    @pl.when(place_ref[0] == 0)
    def _():
        out_ref[...] = product

    @pl.when(place_ref[0] == 1)
    def _():
        swap = exchange_matrix(jnp.int32(1))
        for q in range(tile // REV):
            back = tile - (q + 1) * REV
            out_ref[:, back : back + REV] = mm(
                product[:, q * REV : (q + 1) * REV], swap
            ).astype(bf16)


def output_project(inner, place, gated, squares, gain_row, weights, slots):
    _, rows, cols = gated.shape
    width = weights[0].shape[1]
    shard = width // slots
    tile = min(TILE, shard)
    steps, per_slot = width // tile, shard // tile

    def column(j, place):
        at = place[1] * per_slot + j
        return 0, jnp.where(place[0] == 1, steps - 1 - at, at)

    fixed = lambda shape: pl.BlockSpec(shape, lambda j, place: (0,) * len(shape))
    return pl.pallas_call(
        functools.partial(output_kernel, inner, len(squares)),
        grid_spec=pltpu.PrefetchScalarGridSpec(
            num_scalar_prefetch=1,
            grid=(per_slot,),
            in_specs=[fixed(gated.shape)]
            + [fixed(part.shape) for part in squares]
            + [fixed(gain_row.shape)]
            + [pl.BlockSpec((w.shape[0], tile), column) for w in weights],
            out_specs=pl.BlockSpec((rows, tile), lambda j, place: (0, j)),
            scratch_shapes=[pltpu.VMEM((rows, cols), bf16)],
        ),
        out_shape=jax.ShapeDtypeStruct((rows, shard), bf16),
        name="output_project",
    )(place, gated, *squares, gain_row, *weights)


def incoming_states(total):
    count = lax.axis_size("seq")
    late = lax.axis_index("seq") % 2 == 1
    state = lambda m: m[:STATE].astype(f32)
    keep = lambda m: m[STATE : STATE + 1].astype(f32)
    swap = [(i, i ^ 1) for i in range(count)]
    mine = jnp.where(late, total[0], total[1])
    near = lax.ppermute(jnp.where(late, total[1], total[0]), "seq", swap)
    pair = jnp.concatenate(
        [
            keep(mine) * state(near) + state(mine),
            jnp.broadcast_to(keep(mine) * keep(near), (KEEP_ROWS, total.shape[2])),
        ],
        axis=0,
    ).astype(bf16)
    into, decay = 0.0, 1.0
    for k in range(1, count // 2):
        hop = [(i, i + 2 * k) for i in range(1, count, 2) if i + 2 * k < count]
        hop += [(i, i - 2 * k) for i in range(0, count, 2) if i - 2 * k >= 0]
        got = lax.ppermute(pair, "seq", hop)
        into = into + decay * state(got)
        decay = decay * keep(got)
    across = lax.ppermute(into.astype(bf16), "seq", swap)
    through = (keep(near) * into + state(near)).astype(bf16)
    return jnp.stack([jnp.where(late, through, across), jnp.where(late, across, through)])


def chan_parts(part):
    count = lax.axis_size("chan")
    return [part] + [
        lax.ppermute(part, "chan", [(i, (i + 2 * k) % count) for i in range(count)])
        for k in range(1, count // 2)
    ]


def settled(x):
    def kernel(x_ref, out_ref):
        out_ref[...] = x_ref[...]

    return pl.pallas_call(
        kernel, out_shape=jax.ShapeDtypeStruct(x.shape, x.dtype), name="settled"
    )(x)


def shard_of(rank, turn, count):
    slots = count // 2
    return rank % 2 * slots + (rank // 2 + turn) % slots


def turns(count, back):
    for turn in range(count // 2):
        pairs = [(shard_of(r, turn, count), r) for r in range(count)]
        yield turn, [(b, a) if back else (a, b) for a, b in pairs if a != b]


def gather_strand(hidden, count):
    slots = count // 2
    xs = [hidden] + [lax.ppermute(hidden, "chan", pairs) for _, pairs in turns(count, False)]
    routes = []
    for rank in range(count):
        by_slot = [None] * slots
        for turn in range(slots):
            shard = shard_of(rank, turn, count)
            by_slot[shard % slots] = [0 if shard == rank else 1 + turn]
        routes.append(by_slot)
    return routes, xs


def partner_weights(w, count):
    rows = w.shape[0] // lax.axis_size("seq")
    part = lax.dynamic_slice_in_dim(w, lax.axis_index("seq") * rows, rows, 0)
    part = lax.ppermute(part, "chan", [(i, i ^ 1) for i in range(count)])
    return lax.all_gather(part, "seq", axis=0, tiled=True)


def partner_halves(w, count):
    seq = lax.axis_size("seq")
    rows = w.shape[0] // 2
    part = lax.dynamic_slice_in_dim(w, lax.axis_index("seq") % 2 * rows, rows, 0)
    near = lax.ppermute(part, "chan", [(i, i ^ 1) for i in range(count)])
    far = lax.ppermute(near, "seq", [(i, i ^ 1) for i in range(seq)])
    return near, far


def local(
    hidden, norm_gain, w_values, w_gates, w_control, dt_bias, decay_total, skip_gain, gate_gain,
    w_out, doc_starts,
):
    seq_count, chan_count = lax.axis_size("seq"), lax.axis_size("chan")
    seq_rank, chan_rank = lax.axis_index("seq"), lax.axis_index("chan")
    tokens = hidden.shape[0]
    cols = w_values.shape[1]
    heads = cols // HEAD_DIM
    slots = chan_count // 2

    def mine(a, axis):
        return jnp.concatenate(
            [
                lax.dynamic_slice_in_dim(a, rank * heads, heads, axis)
                for rank in (chan_rank, chan_rank ^ 1)
            ],
            axis,
        )

    lanes = lambda a: jnp.pad(a, ((0, 0), (0, LANES - 2 * heads)))
    routes, xs = gather_strand(hidden, chan_count)
    values_w = (w_values, partner_weights(w_values, chan_count))
    gates_w = (w_gates, partner_weights(w_gates, chan_count))
    out_w = (w_out, *partner_halves(w_out, chan_count))
    swap = [(i, i ^ 1) for i in range(chan_count)]
    gate_row = jnp.concatenate([gate_gain, lax.ppermute(gate_gain, "chan", swap)])[None]
    w_small = jnp.concatenate(
        [w_control[:, : 2 * STATE], lanes(mine(w_control[:, 2 * STATE :], 1))], axis=1
    )
    par = lanes(jnp.stack([mine(dt_bias, 0), mine(decay_total, 0) / (tokens * seq_count)]))
    par = jnp.pad(par, ((0, 6), (0, 0)))
    par = settled(par)
    skip_row = jnp.repeat(mine(skip_gain, 0), HEAD_DIM)[None]
    scalar = lambda v: jnp.reshape(v, (1,)).astype(jnp.int32)
    base, mirror = scalar(seq_rank * tokens), scalar(chan_rank % 2)
    normed, values, control = norm_project(
        routes, xs, scalar(chan_rank), mirror, norm_gain[None], values_w, w_small
    )
    total, pre, cola, colb, rowf, rowb, reach = chunk_states(doc_starts, base, control, values, par)
    into = incoming_states(total)
    active = activated_gates(normed, gates_w)
    near = within(
        doc_starts, base, control, values, skip_row, pre, cola, colb, rowf, rowb
    )
    gated, sums = [], []
    for p in range(PIECES):
        v, squares = carry_gate(control, near, into, reach, active, p, PIECES)
        gated.append(v)
        sums.append(chan_parts(squares))
    total = [0.0] * PIECES
    for turn, pairs in reversed(list(turns(chan_count, True))):
        place = [chan_rank % 2, (chan_rank // 2 + turn) % slots, seq_rank % 2]
        place = jnp.stack(place).astype(jnp.int32)
        kept = shard_of(chan_rank, turn, chan_count) == chan_rank
        for p in range(PIECES):
            part = output_project(
                cols * chan_count, place, gated[p], sums[p], gate_row, out_w, slots
            )
            got = lax.ppermute(part, "chan", pairs)
            total[p] = total[p] + jnp.where(kept, part, got).astype(f32)
    return jnp.concatenate(total, axis=0).astype(bf16)


def solution(mesh):
    in_specs = (
        P("seq", "chan"), P(), P(None, "chan"), P(None, "chan"), P(), P(), P(), P(), P("chan"),
        P("chan", None), P(),
    )
    return jax.shard_map(
        local, mesh=mesh, in_specs=in_specs, out_specs=P("seq", "chan"), check_vma=False
    )
```

```python
import functools

import jax
import jax.numpy as jnp
from jax import lax
from jax.experimental import pallas as pl
from jax.experimental.pallas import tpu as pltpu
from jax.sharding import PartitionSpec as P


HEAD_DIM = 64
STATE = 128
CHUNK = 128
LANES = 128
REV = 256
TILE = 512
KEEP_ROWS = 16
PIECES = (1, 1)


norm_eps = 1e-05
highest = lax.Precision.HIGHEST
f32 = jnp.float32
bf16 = jnp.bfloat16


def mm(a, b):
    return jnp.dot(a, b, preferred_element_type=f32)


def mm_nt(a, b):
    return lax.dot_general(a, b, (((1,), (1,)), ((), ())), preferred_element_type=f32)


def mm_tn(a, b):
    return lax.dot_general(a, b, (((0,), (0,)), ((), ())), preferred_element_type=f32)


def iota(shape, dim):
    return lax.broadcasted_iota(jnp.int32, shape, dim)


def exchange_matrix(mirror):
    row, col = iota((REV, REV), 0), iota((REV, REV), 1)
    return (row == jnp.where(mirror == 1, REV - 1 - col, col)).astype(f32).astype(bf16)


def segment_of(position, starts_ref):
    total = jnp.zeros_like(position)
    for k in range(starts_ref.shape[0]):
        total = total + (position >= starts_ref[k]).astype(jnp.int32)
    return total


def expander(width, first=0):
    row, col = iota((2 * LANES, width), 0), first + iota((2 * LANES, width), 1)
    return ((row % LANES) == (col // HEAD_DIM)).astype(f32).astype(bf16)


def halves(w):
    high = w.astype(bf16)
    low = (w - high.astype(f32)).astype(bf16)
    return jnp.concatenate([high, low], axis=1)


def expand(w, spread):
    return mm(halves(w), spread)


def full(shape):
    return pl.BlockSpec(shape, lambda *_: (0,) * len(shape))


SMEM = pl.BlockSpec(memory_space=pltpu.SMEM)


def norm_project_kernel(routes, rank_ref, mirror_ref, *refs):
    slots, pieces = len(routes[0]), len(routes[0][0])
    xs = refs[: 1 + max(at for by_slot in routes for row in by_slot for at in row)]
    gain_ref, wv_ref, wc_ref, normed_ref, values_ref, control_ref, scr, held, sems = refs[
        len(xs) :
    ]
    half = normed_ref.shape[1]
    blocks = half // REV
    _, tokens, width = held.shape
    rows = tokens // pieces

    @pl.when(pl.program_id(0) == 0)
    def _():
        rank, mirror = rank_ref[0], mirror_ref[0]
        target = lambda j, p: held.at[j, pl.ds(p * rows, rows), :]
        for r, by_slot in enumerate(routes):

            @pl.when(rank == r)
            def _():
                for j in range(slots):
                    for p in range(pieces):
                        pltpu.make_async_copy(
                            xs[by_slot[j][p]], target(j, p), sems.at[j, p]
                        ).start()

        swap = exchange_matrix(mirror)
        squares = jnp.zeros((tokens, 1), f32)
        at = 0
        for j in range(slots):
            for p in range(pieces):
                pltpu.make_async_copy(xs[0], target(j, p), sems.at[j, p]).wait()
            for q in range(width // REV):
                xb = held[j, :, q * REV : (q + 1) * REV]
                wide = xb.astype(f32)
                squares = squares + jnp.sum(wide * wide, axis=1, keepdims=True)
                scr[jnp.where(mirror == 1, blocks - 1 - at, at)] = mm(xb, swap).astype(bf16)
                at += 1
        scale = lax.rsqrt(squares / half + norm_eps)
        for q in range(blocks):
            cols = slice(q * REV, (q + 1) * REV)
            normed_ref[:, cols] = (scr[q].astype(f32) * scale * gain_ref[:, cols]).astype(bf16)
        control_ref[...] = mm(normed_ref[...], wc_ref[...]).astype(bf16)

    values_ref[...] = mm(normed_ref[...], wv_ref[...]).astype(bf16)


def column_half(x, weights, filled=None, activate=False, parity=None):
    tokens, _ = x.shape
    cols = weights[0].shape[1]
    tile = min(TILE, cols)
    steps = cols // tile
    first = 0 if filled is None else steps
    scalars = [] if parity is None else [parity]
    given = [] if filled is None else [filled]

    def kernel(*refs):
        x_ref, *w_refs, out_ref = refs[len(scalars) + len(given) :]
        if scalars:
            product = split_mm(refs[0][0], x_ref, 0, *w_refs)
        else:
            product = mm(x_ref[...], w_refs[0][...])
        product = product.astype(bf16)
        if activate:
            gate = product.astype(f32)
            product = (gate * jax.nn.sigmoid(gate)).astype(bf16)
        out_ref[...] = product

    return pl.pallas_call(
        kernel,
        grid=(steps,),
        in_specs=[SMEM for _ in scalars]
        + [pl.BlockSpec(memory_space=pl.ANY) for _ in given]
        + [full(x.shape)]
        + [pl.BlockSpec((w.shape[0], tile), lambda j: (0, j)) for w in weights],
        out_specs=pl.BlockSpec((tokens, tile), lambda j: (0, j + first)),
        out_shape=jax.ShapeDtypeStruct((tokens, 2 * cols), bf16),
        input_output_aliases={len(scalars): 0} if given else {},
        name="column_half",
    )(*scalars, *given, x, *weights)


def norm_project(routes, xs, rank, mirror, gain, w_values, w_control):
    slots, pieces = len(routes[0]), len(routes[0][0])
    tokens = xs[0].shape[0] * pieces
    half, cols = w_values.shape
    tile = min(TILE, cols)
    steps = cols // tile
    return pl.pallas_call(
        functools.partial(norm_project_kernel, routes),
        grid=(steps,),
        in_specs=[SMEM, SMEM]
        + [pl.BlockSpec(memory_space=pl.ANY) for x in xs]
        + [full(gain.shape), pl.BlockSpec((half, tile), lambda j: (0, j)), full(w_control.shape)],
        out_specs=[
            full((tokens, half)),
            pl.BlockSpec((tokens, tile), lambda j: (0, j)),
            full((tokens, w_control.shape[1])),
        ],
        out_shape=[
            jax.ShapeDtypeStruct((tokens, half), bf16),
            jax.ShapeDtypeStruct((tokens, 2 * cols), bf16),
            jax.ShapeDtypeStruct((tokens, w_control.shape[1]), bf16),
        ],
        scratch_shapes=[
            pltpu.VMEM((half // REV, tokens, REV), bf16),
            pltpu.VMEM((slots, tokens, half // slots), bf16),
            pltpu.SemaphoreType.DMA((slots, pieces)),
        ],
        name="norm_project",
    )(rank, mirror, *xs, gain, w_values, w_control)


def states_kernel(
    starts_ref, base_ref, parity_ref, control_ref, values_ref, par_ref,
    mine_ref, send_ref, pre_ref, cola_ref, colb_ref, rowf_ref, rowb_ref, reach_ref,
    weights_ref, keeps_ref,
):
    tokens, cols = values_ref.shape
    chunks = tokens // CHUNK
    j = pl.program_id(0)

    @pl.when(j == 0)
    def _():
        step_terms(
            starts_ref, base_ref, control_ref, par_ref,
            cola_ref, colb_ref, rowf_ref, rowb_ref, reach_ref, weights_ref, keeps_ref,
        )

    tile = 256
    for at in range(0, cols, tile):
        lanes = slice(at, at + tile)
        spread = expander(tile, j * cols + at)
        lifted = mm(keeps_ref[...], spread)
        wide = values_ref[:, lanes].astype(f32)
        totals = []
        for d, order in enumerate((range(chunks), range(chunks - 1, -1, -1))):
            scaled = (wide * mm(weights_ref[d], spread)).astype(bf16)
            state = jnp.zeros((STATE, tile), f32)
            for i, k in enumerate(order):
                rows = slice(k * CHUNK, (k + 1) * CHUNK)
                pre_ref[d, k, :, lanes] = state.astype(bf16)
                line = d * (chunks + 1) + i
                state = lifted[line : line + 1] * state + mm_tn(
                    control_ref[rows, :STATE], scaled[rows]
                )
            line = d * (chunks + 1) + chunks
            keep = jnp.broadcast_to(lifted[line : line + 1], (KEEP_ROWS, tile))
            totals.append(jnp.concatenate([state, keep], axis=0))
        late = parity_ref[0] == 1
        mine_ref[:, lanes] = jnp.where(late, totals[0], totals[1]).astype(bf16)
        send_ref[:, lanes] = jnp.where(late, totals[1], totals[0]).astype(bf16)


def step_terms(
    starts_ref, base_ref, control_ref, par_ref,
    cola_ref, colb_ref, rowf_ref, rowb_ref, reach_ref, weights_ref, keeps_ref,
):
    tokens = control_ref.shape[0]
    chunks, heads = rowf_ref.shape[:2]
    base = base_ref[0]
    row, col = iota((CHUNK, CHUNK), 0), iota((CHUNK, CHUNK), 1)
    tri = (row >= col).astype(f32)
    seg_at = lambda offset: segment_of(base + jnp.full((1, 1), offset, jnp.int32), starts_ref)
    small, weights = [], [[], []]
    for k in range(chunks):
        rows = slice(k * CHUNK, (k + 1) * CHUNK)
        raw = control_ref[rows, 2 * STATE :].astype(f32) + par_ref[0:1, :]
        step = jnp.maximum(raw, 0.0) + jnp.log1p(jnp.exp(-jnp.abs(raw)))
        log_step = jnp.log(step)
        log_rate = -par_ref[1:2, :] * step
        cum = jnp.dot(tri, log_rate, precision=highest, preferred_element_type=f32)
        before = cum - log_rate
        whole = cum[CHUNK - 1 : CHUNK, :]
        cola_ref[rows, :] = cum
        colb_ref[rows, :] = before
        rowf_ref[k] = jnp.transpose(cum - log_step)[:heads]
        rowb_ref[k] = jnp.transpose(before + log_step)[:heads]
        seg = segment_of(base + k * CHUNK + iota((CHUNK, 1), 0), starts_ref)
        first, last = seg_at(k * CHUNK), seg_at((k + 1) * CHUNK - 1)
        prior, after = seg_at(k * CHUNK - 1), seg_at((k + 1) * CHUNK)
        weights[0].append(jnp.where(seg == last, step * jnp.exp(whole - cum), 0.0))
        weights[1].append(jnp.where(seg == first, step * jnp.exp(before), 0.0))
        keep = jnp.exp(whole)
        keeps = (jnp.where(prior == last, keep, 0.0), jnp.where(first == after, keep, 0.0))
        small.append((seg, cum, whole - before, whole, keeps))
    keep_rows = []
    orders = (range(chunks), range(chunks - 1, -1, -1))
    for d, order in enumerate(orders):
        keep_all = jnp.ones((1, LANES), f32)
        shift = jnp.zeros((1, LANES), f32)
        edge = seg_at(-1) if d == 0 else seg_at(tokens)
        for k in order:
            seg, whole = small[k][0], small[k][3]
            reach_ref[d, k * CHUNK : (k + 1) * CHUNK, :] = jnp.where(
                seg == edge, jnp.exp(small[k][1 + d] + shift), 0.0
            )
            keep_rows.append(small[k][4][d])
            keep_all = keep_all * small[k][4][d]
            shift = shift + whole
        keep_rows.append(keep_all)
    padding = keeps_ref.shape[0] - len(keep_rows)
    keeps_ref[...] = halves(jnp.concatenate(keep_rows + [jnp.zeros((padding, LANES), f32)], axis=0))
    for d in range(2):
        weights_ref[d] = halves(jnp.concatenate(weights[d], axis=0))


def chunk_states(starts, base, parity, control, values, par):
    tokens, cols = values.shape
    chunks, heads = tokens // CHUNK, cols // HEAD_DIM
    shapes = [
        ((STATE + KEEP_ROWS, cols), bf16),
        ((STATE + KEEP_ROWS, cols), bf16),
        ((2, chunks, STATE, cols), bf16),
        ((tokens, LANES), f32),
        ((tokens, LANES), f32),
        ((chunks, heads, CHUNK), f32),
        ((chunks, heads, CHUNK), f32),
        ((2, tokens, LANES), f32),
    ]
    steps = 2 if cols % 512 == 0 else 1
    width = cols // steps
    specs = [
        pl.BlockSpec((STATE + KEEP_ROWS, width), lambda j: (0, j)),
        pl.BlockSpec((STATE + KEEP_ROWS, width), lambda j: (0, j)),
        pl.BlockSpec((2, chunks, STATE, width), lambda j: (0, 0, 0, j)),
    ] + [full(shape) for shape, _ in shapes[3:]]
    return pl.pallas_call(
        states_kernel,
        grid=(steps,),
        in_specs=[
            SMEM, SMEM, SMEM, full(control.shape),
            pl.BlockSpec((tokens, width), lambda j: (0, j)),
            full(par.shape),
        ],
        out_specs=specs,
        out_shape=[jax.ShapeDtypeStruct(s, t) for s, t in shapes],
        scratch_shapes=[
            pltpu.VMEM((2, tokens, 2 * LANES), bf16),
            pltpu.VMEM((-(-2 * (chunks + 1) // 16) * 16, 2 * LANES), bf16),
        ],
        name="chunk_states",
    )(starts, base, parity, control, values, par)


def within_kernel(
    starts_ref, base_ref, control_ref, values_ref, skip_ref,
    pre_ref, cola_ref, colb_ref, rowf_ref, rowb_ref, out_ref,
):
    per_step = values_ref.shape[0] // CHUNK
    spread = expander(values_ref.shape[1])
    for i in range(per_step):
        rows = pl.ds(i * CHUNK, CHUNK)
        start = base_ref[0] + (pl.program_id(0) * per_step + i) * CHUNK
        within_chunk(
            starts_ref, start, control_ref.at[rows], values_ref.at[rows], skip_ref,
            pre_ref.at[:, pl.ds(i, 1)], cola_ref.at[rows], colb_ref.at[rows],
            rowf_ref.at[pl.ds(i, 1)], rowb_ref.at[pl.ds(i, 1)], out_ref.at[:, rows], spread,
        )


def within_chunk(
    starts_ref, start, control_ref, values_ref, skip_ref,
    pre_ref, cola_ref, colb_ref, rowf_ref, rowb_ref, out_ref, spread,
):
    cols = values_ref.shape[1]
    row, col = iota((CHUNK, CHUNK), 0), iota((CHUNK, CHUNK), 1)
    low_lanes = iota((CHUNK, LANES), 1) < HEAD_DIM
    b_in, c_out = control_ref[:, :STATE], control_ref[:, STATE : 2 * STATE]
    seg_col = segment_of(start + iota((CHUNK, 1), 0), starts_ref)
    seg_row = segment_of(start + iota((1, CHUNK), 1), starts_ref)
    prior = segment_of(jnp.full((1, 1), start - 1, jnp.int32), starts_ref)
    after = segment_of(jnp.full((1, 1), start + CHUNK, jnp.int32), starts_ref)
    same = seg_col == seg_row
    lower = row >= col
    scores = mm_nt(c_out, b_in)
    scores_f = jnp.where(lower & same, scores, 0.0)
    scores_b = jnp.where((row <= col) & same, scores, 0.0)
    cum, before = cola_ref[...], colb_ref[...]
    whole = cum[CHUNK - 1 : CHUNK, :]
    far_f = expand(jnp.where(seg_col == prior, jnp.exp(cum), 0.0), spread)
    far_b = expand(jnp.where(seg_col == after, jnp.exp(whole - before), 0.0), spread)
    carry_f = mm(c_out, pre_ref[0, 0]) * far_f
    carry_b = mm(c_out, pre_ref[1, 0]) * far_b
    per_tile = LANES // HEAD_DIM
    for pair in range(cols // LANES):
        lanes = slice(pair * LANES, (pair + 1) * LANES)
        value = values_ref[:, lanes]
        left_f, left_b = [], []
        for h in range(pair * per_tile, (pair + 1) * per_tile):
            gap = jnp.where(
                lower,
                cum[:, h : h + 1] - rowf_ref[0, h : h + 1, :],
                rowb_ref[0, h : h + 1, :] - before[:, h : h + 1],
            )
            weight = jnp.exp(gap)
            left_f.append((weight * scores_f).astype(bf16))
            left_b.append((weight * scores_b).astype(bf16))
        left = jnp.concatenate(
            [jnp.concatenate(left_f, axis=1), jnp.concatenate(left_b, axis=1)], axis=0
        )
        zero = jnp.zeros_like(value)
        right = jnp.concatenate(
            [jnp.where(low_lanes, value, zero), jnp.where(low_lanes, zero, value)], axis=0
        )
        near = mm(left, right)
        direct = value.astype(f32) * skip_ref[:, lanes]
        out_ref[0, :, lanes] = (near[:CHUNK] + carry_f[:, lanes] + direct).astype(bf16)
        out_ref[1, :, lanes] = (near[CHUNK:] + carry_b[:, lanes] + direct).astype(bf16)


def within(starts, base, control, values, skip_row, pre, cola, colb, rowf, rowb):
    tokens, cols = values.shape
    chunks, heads = tokens // CHUNK, cols // HEAD_DIM
    n = 1
    rows = lambda width: pl.BlockSpec((n * CHUNK, width), lambda k: (k, 0))
    return pl.pallas_call(
        within_kernel,
        grid=(chunks // n,),
        in_specs=[
            SMEM, SMEM,
            rows(control.shape[1]), rows(cols), full(skip_row.shape),
            pl.BlockSpec((2, n, STATE, cols), lambda k: (0, k, 0, 0)),
            rows(LANES), rows(LANES),
            pl.BlockSpec((n, heads, CHUNK), lambda k: (k, 0, 0)),
            pl.BlockSpec((n, heads, CHUNK), lambda k: (k, 0, 0)),
        ],
        out_specs=pl.BlockSpec((2, n * CHUNK, cols), lambda k: (0, k, 0)),
        out_shape=jax.ShapeDtypeStruct((2, tokens, cols), bf16),
        name="within_chunk",
    )(starts, base, control, values, skip_row, pre, cola, colb, rowf, rowb)


def gate_kernel(
    parity_ref, control_ref, near_ref, through_ref, across_ref, reach_ref, active_ref,
    out_ref, squares_ref, acc,
):
    tile = active_ref.shape[1]
    rows = active_ref.shape[0]
    j = pl.program_id(0)
    spread = expander(tile, j * tile)
    c_out = control_ref[...]
    active = active_ref[...].astype(f32)
    lane = iota((rows, LANES), 1)
    total = jnp.where(j == 0, 0.0, acc[...])
    for d in range(2):
        state = jnp.where(parity_ref[0] + d == 1, through_ref[...], across_ref[...])
        carry = mm(c_out, state) * expand(reach_ref[d], spread)
        v = (near_ref[d].astype(f32) + carry) * active
        total = total + jnp.where(lane == d, jnp.sum(v * v, axis=1, keepdims=True), 0.0)
        out_ref[d] = v.astype(bf16)
    acc[...] = total

    @pl.when(j == pl.num_programs(0) - 1)
    def _():
        squares_ref[...] = jnp.transpose(acc[...])[:8]


def carry_gate(parity, control, near, into, reach, active, first, rows):
    cols = active.shape[1]
    piece = first // rows
    tile = min(1024, cols)
    return pl.pallas_call(
        gate_kernel,
        grid=(cols // tile,),
        in_specs=[
            SMEM,
            pl.BlockSpec((rows, STATE), lambda j: (piece, 1)),
            pl.BlockSpec((2, rows, tile), lambda j: (0, piece, j)),
            pl.BlockSpec((STATE, tile), lambda j: (0, j)),
            pl.BlockSpec((STATE, tile), lambda j: (0, j)),
            pl.BlockSpec((2, rows, LANES), lambda j: (0, piece, 0)),
            pl.BlockSpec((rows, tile), lambda j: (piece, j)),
        ],
        out_specs=[
            pl.BlockSpec((2, rows, tile), lambda j: (0, 0, j)),
            pl.BlockSpec((8, rows), lambda j: (0, 0)),
        ],
        out_shape=[
            jax.ShapeDtypeStruct((2, rows, cols), bf16),
            jax.ShapeDtypeStruct((8, rows), f32),
        ],
        scratch_shapes=[pltpu.VMEM((rows, LANES), f32)],
        name="carry_gate",
    )(parity, control, near, *into, reach, active)


def split_mm(parity, x_ref, first, near_ref, far_ref):
    rows = near_ref.shape[0]
    cols = lambda half: pl.ds(pl.multiple_of(first + half * rows, rows), rows)
    return mm(x_ref[:, cols(parity)], near_ref[...]) + mm(x_ref[:, cols(1 - parity)], far_ref[...])


def output_kernel(inner, sums, place_ref, gated_ref, *refs):
    squares_refs = refs[:sums]
    gain_ref, wa_ref, near_ref, far_ref, out_ref, combined = refs[sums:]
    rows, tile = out_ref.shape

    @pl.when(pl.program_id(0) == 0)
    def _():
        squares = squares_refs[0][...]
        for other in squares_refs[1:]:
            squares = squares + other[...]
        scale = lax.rsqrt(squares / inner + norm_eps)
        scale = jnp.concatenate([scale, jnp.zeros((LANES - 8, rows), f32)], axis=0)
        scale = jnp.transpose(scale)
        combined[...] = (
            (
                gated_ref[0].astype(f32) * scale[:, 0:1]
                + gated_ref[1].astype(f32) * scale[:, 1:2]
            )
            * gain_ref[...]
        ).astype(bf16)

    cols = wa_ref.shape[0]
    product = mm(combined[:, :cols], wa_ref[...])
    product = (product + split_mm(place_ref[2], combined, cols, near_ref, far_ref)).astype(bf16)

    @pl.when(place_ref[0] == 0)
    def _():
        out_ref[...] = product

    @pl.when(place_ref[0] == 1)
    def _():
        swap = exchange_matrix(jnp.int32(1))
        for q in range(tile // REV):
            back = tile - (q + 1) * REV
            out_ref[:, back : back + REV] = mm(
                product[:, q * REV : (q + 1) * REV], swap
            ).astype(bf16)


def output_project(inner, place, gated, squares, gain_row, weights, slots):
    _, rows, cols = gated.shape
    width = weights[0].shape[1]
    shard = width // slots
    tile = min(TILE, shard)
    steps, per_slot = width // tile, shard // tile

    def column(j, place):
        at = place[1] * per_slot + j
        return 0, jnp.where(place[0] == 1, steps - 1 - at, at)

    fixed = lambda shape: pl.BlockSpec(shape, lambda j, place: (0,) * len(shape))
    return pl.pallas_call(
        functools.partial(output_kernel, inner, len(squares)),
        grid_spec=pltpu.PrefetchScalarGridSpec(
            num_scalar_prefetch=1,
            grid=(per_slot,),
            in_specs=[fixed(gated.shape)]
            + [fixed(part.shape) for part in squares]
            + [fixed(gain_row.shape)]
            + [pl.BlockSpec((w.shape[0], tile), column) for w in weights],
            out_specs=pl.BlockSpec((rows, tile), lambda j, place: (0, j)),
            scratch_shapes=[pltpu.VMEM((rows, cols), bf16)],
        ),
        out_shape=jax.ShapeDtypeStruct((rows, shard), bf16),
        name="output_project",
    )(place, gated, *squares, gain_row, *weights)


def incoming_states(mine, send):
    count = lax.axis_size("seq")
    state = lambda m: m[:STATE].astype(f32)
    keep = lambda m: m[STATE : STATE + 1].astype(f32)
    swap = [(i, i ^ 1) for i in range(count)]
    near = lax.ppermute(send, "seq", swap)
    pair = jnp.concatenate(
        [
            keep(mine) * state(near) + state(mine),
            jnp.broadcast_to(keep(mine) * keep(near), (KEEP_ROWS, mine.shape[1])),
        ],
        axis=0,
    ).astype(bf16)
    into, decay = 0.0, 1.0
    for k in range(1, count // 2):
        hop = [(i, i + 2 * k) for i in range(1, count, 2) if i + 2 * k < count]
        hop += [(i, i - 2 * k) for i in range(0, count, 2) if i - 2 * k >= 0]
        got = lax.ppermute(pair, "seq", hop)
        into = into + decay * state(got)
        decay = decay * keep(got)
    across = lax.ppermute(into.astype(bf16), "seq", swap)
    through = (keep(near) * into + state(near)).astype(bf16)
    return through, across


def chan_parts(part):
    count = lax.axis_size("chan")
    return [part] + [
        lax.ppermute(part, "chan", [(i, (i + 2 * k) % count) for i in range(count)])
        for k in range(1, count // 2)
    ]


def settled(x):
    def kernel(x_ref, out_ref):
        out_ref[...] = x_ref[...]

    return pl.pallas_call(
        kernel, out_shape=jax.ShapeDtypeStruct(x.shape, x.dtype), name="settled"
    )(x)


def shard_of(rank, turn, count):
    slots = count // 2
    return rank % 2 * slots + (rank // 2 + turn) % slots


def turns(count, back):
    for turn in range(count // 2):
        pairs = [(shard_of(r, turn, count), r) for r in range(count)]
        yield turn, [(b, a) if back else (a, b) for a, b in pairs if a != b]


def gather_strand(hidden, count):
    slots = count // 2
    xs = [hidden]
    for turn, pairs in turns(count, False):
        xs.append(lax.ppermute(hidden, "chan", pairs))
    routes = []
    for rank in range(count):
        by_slot = [None] * slots
        for turn in range(slots):
            shard = shard_of(rank, turn, count)
            by_slot[shard % slots] = [0 if shard == rank else 1 + turn]
        routes.append(by_slot)
    return routes, xs


def placed_kernel(chip_ref, *refs):
    *parts, out_ref = refs
    rows = parts[0].shape[0]
    for k, part in enumerate(parts):
        at = pl.multiple_of((chip_ref[0] ^ k) * rows, rows)
        out_ref[pl.ds(at, rows), :] = part[...]


def placed(chip, parts):
    rows, cols = parts[0].shape
    return pl.pallas_call(
        placed_kernel,
        in_specs=[SMEM] + [full(part.shape) for part in parts],
        out_specs=full((rows * len(parts), cols)),
        out_shape=jax.ShapeDtypeStruct((rows * len(parts), cols), bf16),
        name="placed",
    )(chip, *parts)


def partner_weights(w, count):
    seq = lax.axis_size("seq")
    place = lax.axis_index("seq")
    chips = seq // 2
    rows = w.shape[0] // seq
    part = lax.dynamic_slice_in_dim(w, (place % 2 * chips + place // 2) * rows, rows, 0)
    part = lax.ppermute(part, "chan", [(i, i ^ 1) for i in range(count)])
    parts = [part]
    for k in range(1, chips):
        parts.append(lax.ppermute(part, "seq", [(i, i ^ (2 * k)) for i in range(seq)]))
    near = placed(jnp.reshape(place // 2, (1,)).astype(jnp.int32), parts)
    far = lax.ppermute(near, "seq", [(i, i ^ 1) for i in range(seq)])
    return near, far


def partner_halves(w, count):
    seq = lax.axis_size("seq")
    rows = w.shape[0] // 2
    part = lax.dynamic_slice_in_dim(w, lax.axis_index("seq") % 2 * rows, rows, 0)
    near = lax.ppermute(part, "chan", [(i, i ^ 1) for i in range(count)])
    far = lax.ppermute(near, "seq", [(i, i ^ 1) for i in range(seq)])
    return near, far


def local(
    hidden, norm_gain, w_values, w_gates, w_control, dt_bias, decay_total, skip_gain, gate_gain,
    w_out, doc_starts,
):
    seq_count, chan_count = lax.axis_size("seq"), lax.axis_size("chan")
    seq_rank, chan_rank = lax.axis_index("seq"), lax.axis_index("chan")
    tokens = hidden.shape[0]
    cols = w_values.shape[1]
    heads = cols // HEAD_DIM
    slots = chan_count // 2

    def mine(a, axis):
        return jnp.concatenate(
            [
                lax.dynamic_slice_in_dim(a, rank * heads, heads, axis)
                for rank in (chan_rank, chan_rank ^ 1)
            ],
            axis,
        )

    lanes = lambda a: jnp.pad(a, ((0, 0), (0, LANES - 2 * heads)))
    routes, xs = gather_strand(hidden, chan_count)
    values_w = partner_weights(w_values, chan_count)
    gates_w = partner_halves(w_gates, chan_count)
    out_w = (w_out, *partner_weights(w_out, chan_count))
    swap = [(i, i ^ 1) for i in range(chan_count)]
    gate_row = jnp.concatenate([gate_gain, lax.ppermute(gate_gain, "chan", swap)])[None]
    w_small = jnp.concatenate(
        [w_control[:, : 2 * STATE], lanes(mine(w_control[:, 2 * STATE :], 1))], axis=1
    )
    par = lanes(jnp.stack([mine(dt_bias, 0), mine(decay_total, 0) / (tokens * seq_count)]))
    par = jnp.pad(par, ((0, 6), (0, 0)))
    par = settled(par)
    skip_row = jnp.repeat(mine(skip_gain, 0), HEAD_DIM)[None]
    scalar = lambda v: jnp.reshape(v, (1,)).astype(jnp.int32)
    base, mirror = scalar(seq_rank * tokens), scalar(chan_rank % 2)
    parity = scalar(seq_rank % 2)
    normed, values, control = norm_project(
        routes, xs, scalar(chan_rank), mirror, norm_gain[None], w_values, w_small
    )
    values = column_half(normed, values_w, values, False, parity)
    kept, send, pre, cola, colb, rowf, rowb, reach = chunk_states(
        doc_starts, base, parity, control, values, par
    )
    into = incoming_states(kept, send)
    active = column_half(normed, (w_gates,), None, True)
    active = column_half(normed, gates_w, active, True, parity)
    near = within(
        doc_starts, base, control, values, skip_row, pre, cola, colb, rowf, rowb
    )
    gated, sums = [], []
    rows = [tokens * share // sum(PIECES) for share in PIECES]
    for p in range(len(rows)):
        v, squares = carry_gate(parity, control, near, into, reach, active, sum(rows[:p]), rows[p])
        gated.append(v)
        sums.append(chan_parts(squares))
    total = [0.0] * len(rows)
    for turn, pairs in reversed(list(turns(chan_count, True))):
        place = [chan_rank % 2, (chan_rank // 2 + turn) % slots, seq_rank % 2]
        place = jnp.stack(place).astype(jnp.int32)
        kept = shard_of(chan_rank, turn, chan_count) == chan_rank
        for p in range(len(rows)):
            part = output_project(
                cols * chan_count, place, gated[p], sums[p], gate_row, out_w, slots
            )
            got = lax.ppermute(part, "chan", pairs)
            total[p] = total[p] + jnp.where(kept, part, got).astype(f32)
    return jnp.concatenate(total, axis=0).astype(bf16)


def solution(mesh):
    in_specs = (
        P("seq", "chan"), P(), P(None, "chan"), P(None, "chan"), P(), P(), P(), P(), P("chan"),
        P("chan", None), P(),
    )
    return jax.shard_map(
        local, mesh=mesh, in_specs=in_specs, out_specs=P("seq", "chan"), check_vma=False
    )
```

```python
import functools

import jax
import jax.numpy as jnp
from jax import lax
from jax.experimental import pallas as pl
from jax.experimental.pallas import tpu as pltpu
from jax.sharding import PartitionSpec as P


HEAD_DIM = 64
STATE = 128
CHUNK = 128
LANES = 128
REV = 256
TILE = 512
KEEP_ROWS = 16
PIECES = (1, 1)


norm_eps = 1e-05
highest = lax.Precision.HIGHEST
f32 = jnp.float32
bf16 = jnp.bfloat16


def mm(a, b):
    return jnp.dot(a, b, preferred_element_type=f32)


def mm_nt(a, b):
    return lax.dot_general(a, b, (((1,), (1,)), ((), ())), preferred_element_type=f32)


def mm_tn(a, b):
    return lax.dot_general(a, b, (((0,), (0,)), ((), ())), preferred_element_type=f32)


def iota(shape, dim):
    return lax.broadcasted_iota(jnp.int32, shape, dim)


def exchange_matrix(mirror):
    row, col = iota((REV, REV), 0), iota((REV, REV), 1)
    return (row == jnp.where(mirror == 1, REV - 1 - col, col)).astype(f32).astype(bf16)


def segment_of(position, starts_ref):
    total = jnp.zeros_like(position)
    for k in range(starts_ref.shape[0]):
        total = total + (position >= starts_ref[k]).astype(jnp.int32)
    return total


def expander(width, first=0, copies=1):
    row, col = iota((copies * LANES, width), 0), first + iota((copies * LANES, width), 1)
    return ((row % LANES) == (col // HEAD_DIM)).astype(f32).astype(bf16)


def halves(w):
    high = w.astype(bf16)
    low = (w - high.astype(f32)).astype(bf16)
    return jnp.concatenate([high, low], axis=1)


def expand(w, spread):
    return mm(w.astype(bf16), spread)


def full(shape):
    return pl.BlockSpec(shape, lambda *_: (0,) * len(shape))


SMEM = pl.BlockSpec(memory_space=pltpu.SMEM)


def norm_project_kernel(routes, rank_ref, mirror_ref, *refs):
    slots, pieces = len(routes[0]), len(routes[0][0])
    xs = refs[: 1 + max(at for by_slot in routes for row in by_slot for at in row)]
    gain_ref, wv_ref, wc_ref, normed_ref, values_ref, control_ref, scr, held, sems = refs[
        len(xs) :
    ]
    half = normed_ref.shape[1]
    blocks = half // REV
    _, tokens, width = held.shape
    rows = tokens // pieces

    @pl.when(pl.program_id(0) == 0)
    def _():
        rank, mirror = rank_ref[0], mirror_ref[0]
        target = lambda j, p: held.at[j, pl.ds(p * rows, rows), :]
        for r, by_slot in enumerate(routes):

            @pl.when(rank == r)
            def _():
                for j in range(slots):
                    for p in range(pieces):
                        pltpu.make_async_copy(
                            xs[by_slot[j][p]], target(j, p), sems.at[j, p]
                        ).start()

        swap = exchange_matrix(mirror)
        squares = jnp.zeros((tokens, 1), f32)
        at = 0
        for j in range(slots):
            for p in range(pieces):
                pltpu.make_async_copy(xs[0], target(j, p), sems.at[j, p]).wait()
            for q in range(width // REV):
                xb = held[j, :, q * REV : (q + 1) * REV]
                wide = xb.astype(f32)
                squares = squares + jnp.sum(wide * wide, axis=1, keepdims=True)
                scr[jnp.where(mirror == 1, blocks - 1 - at, at)] = mm(xb, swap).astype(bf16)
                at += 1
        scale = lax.rsqrt(squares / half + norm_eps)
        for q in range(blocks):
            cols = slice(q * REV, (q + 1) * REV)
            normed_ref[:, cols] = (scr[q].astype(f32) * scale * gain_ref[:, cols]).astype(bf16)
        control_ref[...] = mm(normed_ref[...], wc_ref[...]).astype(bf16)

    values_ref[...] = mm(normed_ref[...], wv_ref[...]).astype(bf16)


def column_half(x, weights, filled=None, activate=False, parity=None):
    tokens, _ = x.shape
    cols = weights[0].shape[1]
    tile = min(TILE, cols)
    steps = cols // tile
    first = 0 if filled is None else steps
    scalars = [] if parity is None else [parity]
    given = [] if filled is None else [filled]

    def kernel(*refs):
        x_ref, *w_refs, out_ref = refs[len(scalars) + len(given) :]
        if scalars:
            product = split_mm(refs[0][0], x_ref, 0, *w_refs)
        else:
            product = mm(x_ref[...], w_refs[0][...])
        product = product.astype(bf16)
        if activate:
            gate = product.astype(f32)
            product = (gate * jax.nn.sigmoid(gate)).astype(bf16)
        out_ref[...] = product

    return pl.pallas_call(
        kernel,
        grid=(steps,),
        in_specs=[SMEM for _ in scalars]
        + [pl.BlockSpec(memory_space=pl.ANY) for _ in given]
        + [full(x.shape)]
        + [pl.BlockSpec((w.shape[0], tile), lambda j: (0, j)) for w in weights],
        out_specs=pl.BlockSpec((tokens, tile), lambda j: (0, j + first)),
        out_shape=jax.ShapeDtypeStruct((tokens, 2 * cols), bf16),
        input_output_aliases={len(scalars): 0} if given else {},
    )(*scalars, *given, x, *weights)


def norm_project(routes, xs, rank, mirror, gain, w_values, w_control):
    slots, pieces = len(routes[0]), len(routes[0][0])
    tokens = xs[0].shape[0] * pieces
    half, cols = w_values.shape
    tile = min(TILE, cols)
    steps = cols // tile
    return pl.pallas_call(
        functools.partial(norm_project_kernel, routes),
        grid=(steps,),
        in_specs=[SMEM, SMEM]
        + [pl.BlockSpec(memory_space=pl.ANY) for x in xs]
        + [full(gain.shape), pl.BlockSpec((half, tile), lambda j: (0, j)), full(w_control.shape)],
        out_specs=[
            full((tokens, half)),
            pl.BlockSpec((tokens, tile), lambda j: (0, j)),
            full((tokens, w_control.shape[1])),
        ],
        out_shape=[
            jax.ShapeDtypeStruct((tokens, half), bf16),
            jax.ShapeDtypeStruct((tokens, 2 * cols), bf16),
            jax.ShapeDtypeStruct((tokens, w_control.shape[1]), bf16),
        ],
        scratch_shapes=[
            pltpu.VMEM((half // REV, tokens, REV), bf16),
            pltpu.VMEM((slots, tokens, half // slots), bf16),
            pltpu.SemaphoreType.DMA((slots, pieces)),
        ],
    )(rank, mirror, *xs, gain, w_values, w_control)


def states_kernel(
    starts_ref, base_ref, parity_ref, control_ref, values_ref, par_ref,
    mine_ref, send_ref, pre_ref, cola_ref, colb_ref, rowf_ref, rowb_ref, reach_ref,
    weights_ref, keeps_ref,
):
    tokens, cols = values_ref.shape
    chunks = tokens // CHUNK
    j = pl.program_id(0)

    @pl.when(j == 0)
    def _():
        step_terms(
            starts_ref, base_ref, control_ref, par_ref,
            cola_ref, colb_ref, rowf_ref, rowb_ref, reach_ref, weights_ref, keeps_ref,
        )

    tile = 256
    for at in range(0, cols, tile):
        lanes = slice(at, at + tile)
        spread = expander(tile, j * cols + at)
        lifted = mm(keeps_ref[...], expander(tile, j * cols + at, 2))
        wide = values_ref[:, lanes].astype(f32)
        totals = []
        for d, order in enumerate((range(chunks), range(chunks - 1, -1, -1))):
            scaled = (wide * mm(weights_ref[d], spread)).astype(bf16)
            state = jnp.zeros((STATE, tile), f32)
            for i, k in enumerate(order):
                rows = slice(k * CHUNK, (k + 1) * CHUNK)
                pre_ref[d, k, :, lanes] = state.astype(bf16)
                line = d * (chunks + 1) + i
                state = lifted[line : line + 1] * state + mm_tn(
                    control_ref[rows, :STATE], scaled[rows]
                )
            line = d * (chunks + 1) + chunks
            keep = jnp.broadcast_to(lifted[line : line + 1], (KEEP_ROWS, tile))
            totals.append(jnp.concatenate([state, keep], axis=0))
        late = parity_ref[0] == 1
        mine_ref[:, lanes] = jnp.where(late, totals[0], totals[1]).astype(bf16)
        send_ref[:, lanes] = jnp.where(late, totals[1], totals[0]).astype(bf16)


def step_terms(
    starts_ref, base_ref, control_ref, par_ref,
    cola_ref, colb_ref, rowf_ref, rowb_ref, reach_ref, weights_ref, keeps_ref,
):
    tokens = control_ref.shape[0]
    chunks, heads = rowf_ref.shape[:2]
    base = base_ref[0]
    row, col = iota((CHUNK, CHUNK), 0), iota((CHUNK, CHUNK), 1)
    tri = (row >= col).astype(f32)
    seg_at = lambda offset: segment_of(base + jnp.full((1, 1), offset, jnp.int32), starts_ref)
    small, weights = [], [[], []]
    for k in range(chunks):
        rows = slice(k * CHUNK, (k + 1) * CHUNK)
        raw = control_ref[rows, 2 * STATE :].astype(f32) + par_ref[0:1, :]
        step = jnp.maximum(raw, 0.0) + jnp.log1p(jnp.exp(-jnp.abs(raw)))
        log_step = jnp.log(step)
        log_rate = -par_ref[1:2, :] * step
        cum = jnp.dot(tri, log_rate, precision=highest, preferred_element_type=f32)
        before = cum - log_rate
        whole = cum[CHUNK - 1 : CHUNK, :]
        cola_ref[rows, :] = cum
        colb_ref[rows, :] = before
        rowf_ref[k] = jnp.transpose(cum - log_step)[:heads]
        rowb_ref[k] = jnp.transpose(before + log_step)[:heads]
        seg = segment_of(base + k * CHUNK + iota((CHUNK, 1), 0), starts_ref)
        first, last = seg_at(k * CHUNK), seg_at((k + 1) * CHUNK - 1)
        prior, after = seg_at(k * CHUNK - 1), seg_at((k + 1) * CHUNK)
        weights[0].append(jnp.where(seg == last, step * jnp.exp(whole - cum), 0.0))
        weights[1].append(jnp.where(seg == first, step * jnp.exp(before), 0.0))
        keep = jnp.exp(whole)
        keeps = (jnp.where(prior == last, keep, 0.0), jnp.where(first == after, keep, 0.0))
        small.append((seg, cum, whole - before, whole, keeps))
    keep_rows = []
    orders = (range(chunks), range(chunks - 1, -1, -1))
    for d, order in enumerate(orders):
        keep_all = jnp.ones((1, LANES), f32)
        shift = jnp.zeros((1, LANES), f32)
        edge = seg_at(-1) if d == 0 else seg_at(tokens)
        for k in order:
            seg, whole = small[k][0], small[k][3]
            reach_ref[d, k * CHUNK : (k + 1) * CHUNK, :] = jnp.where(
                seg == edge, jnp.exp(small[k][1 + d] + shift), 0.0
            )
            keep_rows.append(small[k][4][d])
            keep_all = keep_all * small[k][4][d]
            shift = shift + whole
        keep_rows.append(keep_all)
    padding = keeps_ref.shape[0] - len(keep_rows)
    keeps_ref[...] = halves(jnp.concatenate(keep_rows + [jnp.zeros((padding, LANES), f32)], axis=0))
    for d in range(2):
        weights_ref[d] = jnp.concatenate(weights[d], axis=0).astype(bf16)


def chunk_states(starts, base, parity, control, values, par):
    tokens, cols = values.shape
    chunks, heads = tokens // CHUNK, cols // HEAD_DIM
    shapes = [
        ((STATE + KEEP_ROWS, cols), bf16),
        ((STATE + KEEP_ROWS, cols), bf16),
        ((2, chunks, STATE, cols), bf16),
        ((tokens, LANES), f32),
        ((tokens, LANES), f32),
        ((chunks, heads, CHUNK), f32),
        ((chunks, heads, CHUNK), f32),
        ((2, tokens, LANES), f32),
    ]
    steps = 2 if cols % 512 == 0 else 1
    width = cols // steps
    specs = [
        pl.BlockSpec((STATE + KEEP_ROWS, width), lambda j: (0, j)),
        pl.BlockSpec((STATE + KEEP_ROWS, width), lambda j: (0, j)),
        pl.BlockSpec((2, chunks, STATE, width), lambda j: (0, 0, 0, j)),
    ] + [full(shape) for shape, _ in shapes[3:]]
    return pl.pallas_call(
        states_kernel,
        grid=(steps,),
        in_specs=[
            SMEM, SMEM, SMEM, full(control.shape),
            pl.BlockSpec((tokens, width), lambda j: (0, j)),
            full(par.shape),
        ],
        out_specs=specs,
        out_shape=[jax.ShapeDtypeStruct(s, t) for s, t in shapes],
        scratch_shapes=[
            pltpu.VMEM((2, tokens, LANES), bf16),
            pltpu.VMEM((-(-2 * (chunks + 1) // 16) * 16, 2 * LANES), bf16),
        ],
    )(starts, base, parity, control, values, par)


def within_kernel(
    starts_ref, base_ref, control_ref, values_ref, skip_ref,
    pre_ref, cola_ref, colb_ref, rowf_ref, rowb_ref, out_ref,
):
    per_step = values_ref.shape[0] // CHUNK
    spread = expander(values_ref.shape[1])
    for i in range(per_step):
        rows = pl.ds(i * CHUNK, CHUNK)
        start = base_ref[0] + (pl.program_id(0) * per_step + i) * CHUNK
        within_chunk(
            starts_ref, start, control_ref.at[rows], values_ref.at[rows], skip_ref,
            pre_ref.at[:, pl.ds(i, 1)], cola_ref.at[rows], colb_ref.at[rows],
            rowf_ref.at[pl.ds(i, 1)], rowb_ref.at[pl.ds(i, 1)], out_ref.at[:, rows], spread,
        )


def within_chunk(
    starts_ref, start, control_ref, values_ref, skip_ref,
    pre_ref, cola_ref, colb_ref, rowf_ref, rowb_ref, out_ref, spread,
):
    cols = values_ref.shape[1]
    row, col = iota((CHUNK, CHUNK), 0), iota((CHUNK, CHUNK), 1)
    low_lanes = iota((CHUNK, LANES), 1) < HEAD_DIM
    b_in, c_out = control_ref[:, :STATE], control_ref[:, STATE : 2 * STATE]
    seg_col = segment_of(start + iota((CHUNK, 1), 0), starts_ref)
    seg_row = segment_of(start + iota((1, CHUNK), 1), starts_ref)
    prior = segment_of(jnp.full((1, 1), start - 1, jnp.int32), starts_ref)
    after = segment_of(jnp.full((1, 1), start + CHUNK, jnp.int32), starts_ref)
    same = seg_col == seg_row
    lower = row >= col
    scores = mm_nt(c_out, b_in)
    scores_f = jnp.where(lower & same, scores, 0.0)
    scores_b = jnp.where((row <= col) & same, scores, 0.0)
    cum, before = cola_ref[...], colb_ref[...]
    whole = cum[CHUNK - 1 : CHUNK, :]
    far_f = expand(jnp.where(seg_col == prior, jnp.exp(cum), 0.0), spread)
    far_b = expand(jnp.where(seg_col == after, jnp.exp(whole - before), 0.0), spread)
    carry_f = mm(c_out, pre_ref[0, 0]) * far_f
    carry_b = mm(c_out, pre_ref[1, 0]) * far_b
    per_tile = LANES // HEAD_DIM
    for pair in range(cols // LANES):
        lanes = slice(pair * LANES, (pair + 1) * LANES)
        value = values_ref[:, lanes]
        left_f, left_b = [], []
        for h in range(pair * per_tile, (pair + 1) * per_tile):
            gap = jnp.where(
                lower,
                cum[:, h : h + 1] - rowf_ref[0, h : h + 1, :],
                rowb_ref[0, h : h + 1, :] - before[:, h : h + 1],
            )
            weight = jnp.exp(gap)
            left_f.append((weight * scores_f).astype(bf16))
            left_b.append((weight * scores_b).astype(bf16))
        left = jnp.concatenate(
            [jnp.concatenate(left_f, axis=1), jnp.concatenate(left_b, axis=1)], axis=0
        )
        zero = jnp.zeros_like(value)
        right = jnp.concatenate(
            [jnp.where(low_lanes, value, zero), jnp.where(low_lanes, zero, value)], axis=0
        )
        near = mm(left, right)
        direct = value.astype(f32) * skip_ref[:, lanes]
        out_ref[0, :, lanes] = (near[:CHUNK] + carry_f[:, lanes] + direct).astype(bf16)
        out_ref[1, :, lanes] = (near[CHUNK:] + carry_b[:, lanes] + direct).astype(bf16)


def within(starts, base, control, values, skip_row, pre, cola, colb, rowf, rowb):
    tokens, cols = values.shape
    chunks, heads = tokens // CHUNK, cols // HEAD_DIM
    n = 1
    rows = lambda width: pl.BlockSpec((n * CHUNK, width), lambda k: (k, 0))
    return pl.pallas_call(
        within_kernel,
        grid=(chunks // n,),
        in_specs=[
            SMEM, SMEM,
            rows(control.shape[1]), rows(cols), full(skip_row.shape),
            pl.BlockSpec((2, n, STATE, cols), lambda k: (0, k, 0, 0)),
            rows(LANES), rows(LANES),
            pl.BlockSpec((n, heads, CHUNK), lambda k: (k, 0, 0)),
            pl.BlockSpec((n, heads, CHUNK), lambda k: (k, 0, 0)),
        ],
        out_specs=pl.BlockSpec((2, n * CHUNK, cols), lambda k: (0, k, 0)),
        out_shape=jax.ShapeDtypeStruct((2, tokens, cols), bf16),
    )(starts, base, control, values, skip_row, pre, cola, colb, rowf, rowb)


def gate_kernel(
    parity_ref, control_ref, near_ref, through_ref, across_ref, reach_ref, active_ref,
    out_ref, squares_ref, acc,
):
    tile = active_ref.shape[1]
    rows = active_ref.shape[0]
    j = pl.program_id(0)
    spread = expander(tile, j * tile)
    c_out = control_ref[...]
    active = active_ref[...].astype(f32)
    lane = iota((rows, LANES), 1)
    total = jnp.where(j == 0, 0.0, acc[...])
    for d in range(2):
        state = jnp.where(parity_ref[0] + d == 1, through_ref[...], across_ref[...])
        carry = mm(c_out, state) * expand(reach_ref[d], spread)
        v = (near_ref[d].astype(f32) + carry) * active
        total = total + jnp.where(lane == d, jnp.sum(v * v, axis=1, keepdims=True), 0.0)
        out_ref[d] = v.astype(bf16)
    acc[...] = total

    @pl.when(j == pl.num_programs(0) - 1)
    def _():
        squares_ref[...] = jnp.transpose(acc[...])[:8]


def carry_gate(parity, control, near, into, reach, active, first, rows):
    cols = active.shape[1]
    piece = first // rows
    tile = min(1024, cols)
    return pl.pallas_call(
        gate_kernel,
        grid=(cols // tile,),
        in_specs=[
            SMEM,
            pl.BlockSpec((rows, STATE), lambda j: (piece, 1)),
            pl.BlockSpec((2, rows, tile), lambda j: (0, piece, j)),
            pl.BlockSpec((STATE, tile), lambda j: (0, j)),
            pl.BlockSpec((STATE, tile), lambda j: (0, j)),
            pl.BlockSpec((2, rows, LANES), lambda j: (0, piece, 0)),
            pl.BlockSpec((rows, tile), lambda j: (piece, j)),
        ],
        out_specs=[
            pl.BlockSpec((2, rows, tile), lambda j: (0, 0, j)),
            pl.BlockSpec((8, rows), lambda j: (0, 0)),
        ],
        out_shape=[
            jax.ShapeDtypeStruct((2, rows, cols), bf16),
            jax.ShapeDtypeStruct((8, rows), f32),
        ],
        scratch_shapes=[pltpu.VMEM((rows, LANES), f32)],
    )(parity, control, near, *into, reach, active)


def split_mm(parity, x_ref, first, near_ref, far_ref):
    rows = near_ref.shape[0]
    cols = lambda half: pl.ds(pl.multiple_of(first + half * rows, rows), rows)
    return mm(x_ref[:, cols(parity)], near_ref[...]) + mm(x_ref[:, cols(1 - parity)], far_ref[...])


def output_kernel(inner, sums, place_ref, gated_ref, *refs):
    squares_refs = refs[:sums]
    gain_ref, wa_ref, near_ref, far_ref, out_ref, combined = refs[sums:]
    rows, tile = out_ref.shape

    @pl.when(pl.program_id(0) == 0)
    def _():
        squares = squares_refs[0][...]
        for other in squares_refs[1:]:
            squares = squares + other[...]
        scale = lax.rsqrt(squares / inner + norm_eps)
        scale = jnp.concatenate([scale, jnp.zeros((LANES - 8, rows), f32)], axis=0)
        scale = jnp.transpose(scale)
        combined[...] = (
            (
                gated_ref[0].astype(f32) * scale[:, 0:1]
                + gated_ref[1].astype(f32) * scale[:, 1:2]
            )
            * gain_ref[...]
        ).astype(bf16)

    cols = wa_ref.shape[0]
    product = mm(combined[:, :cols], wa_ref[...])
    product = (product + split_mm(place_ref[2], combined, cols, near_ref, far_ref)).astype(bf16)

    @pl.when(place_ref[0] == 0)
    def _():
        out_ref[...] = product

    @pl.when(place_ref[0] == 1)
    def _():
        swap = exchange_matrix(jnp.int32(1))
        for q in range(tile // REV):
            back = tile - (q + 1) * REV
            out_ref[:, back : back + REV] = mm(
                product[:, q * REV : (q + 1) * REV], swap
            ).astype(bf16)


def output_project(inner, place, gated, squares, gain_row, weights, slots):
    _, rows, cols = gated.shape
    width = weights[0].shape[1]
    shard = width // slots
    tile = min(TILE, shard)
    steps, per_slot = width // tile, shard // tile

    def column(j, place):
        at = place[1] * per_slot + j
        return 0, jnp.where(place[0] == 1, steps - 1 - at, at)

    fixed = lambda shape: pl.BlockSpec(shape, lambda j, place: (0,) * len(shape))
    return pl.pallas_call(
        functools.partial(output_kernel, inner, len(squares)),
        grid_spec=pltpu.PrefetchScalarGridSpec(
            num_scalar_prefetch=1,
            grid=(per_slot,),
            in_specs=[fixed(gated.shape)]
            + [fixed(part.shape) for part in squares]
            + [fixed(gain_row.shape)]
            + [pl.BlockSpec((w.shape[0], tile), column) for w in weights],
            out_specs=pl.BlockSpec((rows, tile), lambda j, place: (0, j)),
            scratch_shapes=[pltpu.VMEM((rows, cols), bf16)],
        ),
        out_shape=jax.ShapeDtypeStruct((rows, shard), bf16),
    )(place, gated, *squares, gain_row, *weights)


def joined_kernel(near_ref, *refs):
    *got, into_ref, through_ref = refs
    state = lambda ref: ref[:STATE, :].astype(f32)
    keep = lambda ref: ref[STATE : STATE + 1, :].astype(f32)
    into = state(got[-1])
    for ref in reversed(got[:-1]):
        into = state(ref) + keep(ref) * into
    into_ref[...] = into.astype(bf16)
    through_ref[...] = (keep(near_ref) * into + state(near_ref)).astype(bf16)


def joined(near, got):
    depth, cols = near.shape
    width = cols // 2
    block = lambda rows: pl.BlockSpec((rows, width), lambda j: (0, j))
    return pl.pallas_call(
        joined_kernel,
        grid=(2,),
        in_specs=[block(depth) for _ in range(1 + len(got))],
        out_specs=[block(STATE)] * 2,
        out_shape=[jax.ShapeDtypeStruct((STATE, cols), bf16)] * 2,
    )(near, *got)


def incoming_states(mine, send):
    count = lax.axis_size("seq")
    state = lambda m: m[:STATE].astype(f32)
    keep = lambda m: m[STATE : STATE + 1].astype(f32)
    swap = [(i, i ^ 1) for i in range(count)]
    near = lax.ppermute(send, "seq", swap)
    pair = jnp.concatenate(
        [
            keep(mine) * state(near) + state(mine),
            jnp.broadcast_to(keep(mine) * keep(near), (KEEP_ROWS, mine.shape[1])),
        ],
        axis=0,
    ).astype(bf16)
    got = []
    for k in range(1, count // 2):
        hop = [(i, i + 2 * k) for i in range(1, count, 2) if i + 2 * k < count]
        hop += [(i, i - 2 * k) for i in range(0, count, 2) if i - 2 * k >= 0]
        got.append(lax.ppermute(pair, "seq", hop))
    into, through = joined(near, got)
    across = lax.ppermute(into, "seq", swap)
    return through, across


def chan_parts(part):
    count = lax.axis_size("chan")
    return [part] + [
        lax.ppermute(part, "chan", [(i, (i + 2 * k) % count) for i in range(count)])
        for k in range(1, count // 2)
    ]


def settled(x, *ready):
    def kernel(x_ref, *refs):
        refs[-1][...] = x_ref[...]

    return pl.pallas_call(
        kernel,
        in_specs=[full(x.shape)] + [pl.BlockSpec(memory_space=pl.ANY) for _ in ready],
        out_specs=full(x.shape),
        out_shape=jax.ShapeDtypeStruct(x.shape, x.dtype),
    )(x, *ready)


def shard_of(rank, turn, count):
    slots = count // 2
    return rank % 2 * slots + (rank // 2 + turn) % slots


def turns(count, back):
    for turn in range(count // 2):
        pairs = [(shard_of(r, turn, count), r) for r in range(count)]
        yield turn, [(b, a) if back else (a, b) for a, b in pairs if a != b]


def gather_strand(hidden, count):
    slots = count // 2
    xs = [hidden]
    for turn, pairs in turns(count, False):
        xs.append(lax.ppermute(hidden, "chan", pairs))
    routes = []
    for rank in range(count):
        by_slot = [None] * slots
        for turn in range(slots):
            shard = shard_of(rank, turn, count)
            by_slot[shard % slots] = [0 if shard == rank else 1 + turn]
        routes.append(by_slot)
    return routes, xs


def placed_kernel(chip_ref, *refs):
    *parts, out_ref = refs
    rows = parts[0].shape[0]
    for k, part in enumerate(parts):
        at = pl.multiple_of((chip_ref[0] ^ k) * rows, rows)
        out_ref[pl.ds(at, rows), :] = part[...]


def placed(chip, parts):
    rows, cols = parts[0].shape
    return pl.pallas_call(
        placed_kernel,
        in_specs=[SMEM] + [full(part.shape) for part in parts],
        out_specs=full((rows * len(parts), cols)),
        out_shape=jax.ShapeDtypeStruct((rows * len(parts), cols), bf16),
    )(chip, *parts)


def partner_weights(w, count):
    seq = lax.axis_size("seq")
    place = lax.axis_index("seq")
    chips = seq // 2
    rows = w.shape[0] // seq
    part = lax.dynamic_slice_in_dim(w, (place % 2 * chips + place // 2) * rows, rows, 0)
    part = lax.ppermute(part, "chan", [(i, i ^ 1) for i in range(count)])
    parts = [part]
    for k in range(1, chips):
        parts.append(lax.ppermute(part, "seq", [(i, i ^ (2 * k)) for i in range(seq)]))
    near = placed(jnp.reshape(place // 2, (1,)).astype(jnp.int32), parts)
    far = lax.ppermute(near, "seq", [(i, i ^ 1) for i in range(seq)])
    return near, far


def partner_halves(w, count):
    seq = lax.axis_size("seq")
    rows = w.shape[0] // 2
    part = lax.dynamic_slice_in_dim(w, lax.axis_index("seq") % 2 * rows, rows, 0)
    near = lax.ppermute(part, "chan", [(i, i ^ 1) for i in range(count)])
    far = lax.ppermute(near, "seq", [(i, i ^ 1) for i in range(seq)])
    return near, far


def local(
    hidden, norm_gain, w_values, w_gates, w_control, dt_bias, decay_total, skip_gain, gate_gain,
    w_out, doc_starts,
):
    seq_count, chan_count = lax.axis_size("seq"), lax.axis_size("chan")
    seq_rank, chan_rank = lax.axis_index("seq"), lax.axis_index("chan")
    tokens = hidden.shape[0]
    cols = w_values.shape[1]
    heads = cols // HEAD_DIM
    slots = chan_count // 2

    def mine(a, axis):
        return jnp.concatenate(
            [
                lax.dynamic_slice_in_dim(a, rank * heads, heads, axis)
                for rank in (chan_rank, chan_rank ^ 1)
            ],
            axis,
        )

    lanes = lambda a: jnp.pad(a, ((0, 0), (0, LANES - 2 * heads)))
    routes, xs = gather_strand(hidden, chan_count)
    values_w = partner_weights(w_values, chan_count)
    gates_w = partner_halves(w_gates, chan_count)
    out_w = (w_out, *partner_weights(w_out, chan_count))
    swap = [(i, i ^ 1) for i in range(chan_count)]
    gate_row = jnp.concatenate([gate_gain, lax.ppermute(gate_gain, "chan", swap)])[None]
    w_small = jnp.concatenate(
        [w_control[:, : 2 * STATE], lanes(mine(w_control[:, 2 * STATE :], 1))], axis=1
    )
    par = lanes(jnp.stack([mine(dt_bias, 0), mine(decay_total, 0) / (tokens * seq_count)]))
    par = jnp.pad(par, ((0, 6), (0, 0)))
    places = [
        jnp.stack([chan_rank % 2, (chan_rank // 2 + turn) % slots, seq_rank % 2]).astype(jnp.int32)
        for turn in range(slots)
    ]
    par = settled(par)
    skip_row = jnp.repeat(mine(skip_gain, 0), HEAD_DIM)[None]
    scalar = lambda v: jnp.reshape(v, (1,)).astype(jnp.int32)
    base, mirror = scalar(seq_rank * tokens), scalar(chan_rank % 2)
    parity = scalar(seq_rank % 2)
    par = settled(par, w_small, skip_row, base, mirror, parity, *places)
    normed, values, control = norm_project(
        routes, xs, scalar(chan_rank), mirror, norm_gain[None], w_values, w_small
    )
    values = column_half(normed, values_w, values, False, parity)
    kept, send, pre, cola, colb, rowf, rowb, reach = chunk_states(
        doc_starts, base, parity, control, values, par
    )
    into = incoming_states(kept, send)
    active = column_half(normed, (w_gates,), None, True)
    active = column_half(normed, gates_w, active, True, parity)
    near = within(
        doc_starts, base, control, values, skip_row, pre, cola, colb, rowf, rowb
    )
    gated, sums = [], []
    rows = [tokens * share // sum(PIECES) for share in PIECES]
    for p in range(len(rows)):
        v, squares = carry_gate(parity, control, near, into, reach, active, sum(rows[:p]), rows[p])
        gated.append(v)
        sums.append(chan_parts(squares))
    total = [0.0] * len(rows)
    for turn, pairs in reversed(list(turns(chan_count, True))):
        place = places[turn]
        kept = shard_of(chan_rank, turn, chan_count) == chan_rank
        for p in range(len(rows)):
            part = output_project(
                cols * chan_count, place, gated[p], sums[p], gate_row, out_w, slots
            )
            got = lax.ppermute(part, "chan", pairs)
            total[p] = total[p] + jnp.where(kept, part, got).astype(f32)
    return jnp.concatenate(total, axis=0).astype(bf16)


def solution(mesh):
    in_specs = (
        P("seq", "chan"), P(), P(None, "chan"), P(None, "chan"), P(), P(), P(), P(), P("chan"),
        P("chan", None), P(),
    )
    return jax.shard_map(
        local, mesh=mesh, in_specs=in_specs, out_specs=P("seq", "chan"), check_vma=False
    )
```
